512 devices in a mesh: dp: 16 (over z, core), seq: 32 (over x, y).
Axes of the slice: x: 4, y: 8, z: 8, core: 2. Of those that a mesh axis runs over, the one named last changes fastest.
Arguments:
- inputs: bfloat16 [16, 4096, 4096], P('dp', 'seq'), may hold values from -6 to 6
- out_grads: bfloat16 [16, 4096, 14336], P('dp', 'seq'), may hold values from -6 to 6
- valid: int32 [16, 4096], P('dp', 'seq'), may hold values 0 or 1
- doc_blocks: int32 [16, 4], P('dp'), may hold values from 1 to 16, 32 in all within a row
- doc_ids: int32 [64], replicated, may hold values from 0 to 63, each once
- proj_in: bfloat16 [4096, 64], P('seq'), may hold values from -0.09375 to 0.09375
- proj_out: bfloat16 [14336, 64], P('seq'), may hold values from -0.046875 to 0.046875
- test_grads: bfloat16 [1024, 4096], P('seq'), may hold values from -192 to 192
Outputs:
- scores: float32 [64, 1024], P(None, 'seq')
The draws below stay inside these ranges and needn't reach their ends.
Inputs may be any that keep to these rules, and one draw needn't show every extreme that they name: `doc_blocks`: each group's lengths sum to 32; the largest is 16 in every group. `doc_ids`: every document number appears once.
All inputs are finite; a program needn't handle non-finite values. No bound on the sum of `valid` on one device may be relied on, other than what follows from the above.
Results may differ from the reference program's by a relative error of at most 0.0003.
Values may be sent and summed in bfloat16 or wider, within the bound.
A program may use at most 64 MiB of HBM per device.

```python
import math
import jax
import jax.numpy as jnp
import numpy as np
from jax import lax

D = 4096
FF = 14336
PROJ_IN = 64
PROJ_OUT = 64
FEAT = 4096
BLOCK = 128
DOC_GRP = 4
GROUPS = 16
SEQ_TOK = 4096
BLK_GRP = 32
MOST = 16
NDOCS = 64
NTEST = 1024


def touch_ends(values, key, least, top_value):
    extent = values.shape
    index_at = [jax.random.randint(jax.random.fold_in(key, axis), (), 0, extent[axis]) for axis in range(len(extent))]
    values = values.at[tuple(index_at)].set(least)
    longest = extent.index(max(extent))
    index_at[longest] = (index_at[longest] + 1) % extent[longest]
    return values.at[tuple(index_at)].set(top_value)


def block_scale(key, shape, split, smallest, top_value):
    gain = 1.0
    for position, shards_of in split:
        heights = jax.random.uniform(jax.random.fold_in(jax.random.fold_in(key, 6), position), (shards_of,), jnp.float32, smallest / len(split), top_value / len(split))
        gain = gain * jnp.repeat(jnp.exp(heights), shape[position] // shards_of).reshape((-1,) + (1,) * (len(shape) - 1 - position))
    return gain


def profile(amount, total, most, slope):
    portions = [(1 << 20) // math.isqrt(grade ** slope) + 1 for grade in range(2, amount + 1)]
    surplus, holding = total - most - (amount - 1), [1] * (amount - 1)
    while surplus > 0:
        free = [i for i in range(amount - 1) if holding[i] < most]
        mass, budget = sum([portions[i] for i in free]), surplus
        for i in free:
            more = min(most - holding[i], max(1, budget * portions[i] // mass), surplus)
            holding[i] = holding[i] + more
            surplus = surplus - more
    return np.array([most] + holding)


def uneven_parts(own_key, amount, total, reach, lean):
    if amount == 2:
        one = jax.random.randint(own_key, (), max(1, total - reach), min(reach, total - 1) + 1)
        return jnp.stack([one, total - one])
    sizes = jnp.asarray(profile(amount, total, reach, lean), jnp.int32)
    pairs = (amount - 1) // 2
    giver, receiver = sizes[1:1 + 2 * pairs:2], sizes[2:2 + 2 * pairs:2]
    margin = jnp.minimum(giver - 1, reach - receiver)
    moved = jax.random.randint(jax.random.fold_in(own_key, 1), (pairs,), 0, 1 << 20) % (margin + 1)
    sizes = sizes.at[1:1 + 2 * pairs:2].set(giver - moved).at[2:2 + 2 * pairs:2].set(receiver + moved)
    return sizes[jax.random.permutation(jax.random.fold_in(own_key, 2), amount)]


def normal_values(rng, dims, spread, reach, split=(), kind=jnp.bfloat16):
    array = jax.random.normal(rng, dims, jnp.float32) * spread
    if len(split) > 0:
        array = block_scale(rng, dims, split, -0.22, 0.18) * array
    return jnp.clip(array, min=-reach, max=reach).astype(kind)


def setup_inputs(seed: int = 0) -> dict:
    key_of = jax.random.split(jax.random.key(seed), 9)
    return {
        "inputs": normal_values(key_of[0], (GROUPS, SEQ_TOK, D), 1.0, 6.0, ((0, 16), (1, 32))),
        "out_grads": normal_values(key_of[1], (GROUPS, SEQ_TOK, FF), 1.0, 6.0, ((0, 16), (1, 32))),
        "valid": touch_ends((jax.random.randint(key_of[2], (GROUPS, SEQ_TOK), 0, 8) < 7).astype(jnp.int32), jax.random.fold_in(key_of[2], 1), 0, 1),
        "doc_blocks": jax.vmap(lambda own: uneven_parts(own, DOC_GRP, BLK_GRP, MOST, 2))(jax.random.split(key_of[3], GROUPS)).reshape((GROUPS, DOC_GRP)).astype(jnp.int32),
        "doc_ids": jax.random.permutation(key_of[4], NDOCS).astype(jnp.int32),
        "proj_in": normal_values(key_of[5], (D, PROJ_IN), D ** -0.5, 0.09375, ((0, 32),)),
        "proj_out": normal_values(key_of[6], (FF, PROJ_OUT), FF ** -0.5, 0.046875, ((0, 32),)),
        "test_grads": normal_values(key_of[7], (NTEST, FEAT), 32.0, 192.0, ((0, 32),)),
    }


def group_grads(args, proj_in, proj_out):
    inputs, out_grads, valid, blocks = args
    px = jnp.dot(inputs.astype(jnp.float32), proj_in.astype(jnp.float32), preferred_element_type=jnp.float32)
    pg = jnp.dot(out_grads.astype(jnp.float32), proj_out.astype(jnp.float32), preferred_element_type=jnp.float32)
    ends = jnp.cumsum(blocks).astype(jnp.int32)
    blk = (jnp.arange(SEQ_TOK, dtype=jnp.int32) // BLOCK).astype(jnp.int32)
    owner = jnp.sum((blk[:, None] >= ends[None, :]).astype(jnp.int32), axis=1)
    onehot = ((owner[:, None] == jnp.arange(DOC_GRP, dtype=jnp.int32)[None, :]) & (valid[:, None] == 1)).astype(jnp.float32)
    weighted = (onehot[:, :, None] * pg[:, None, :]).reshape(SEQ_TOK, DOC_GRP * PROJ_OUT)
    summed = jnp.dot(weighted.T, px, precision=lax.Precision.HIGHEST)
    return summed.reshape(DOC_GRP, FEAT)

def reference(inputs, out_grads, valid, doc_blocks, doc_ids, proj_in, proj_out, test_grads):
    per_group = lax.map(lambda a: group_grads(a, proj_in, proj_out), (inputs, out_grads, valid, doc_blocks))
    doc_grads = per_group.reshape(NDOCS, FEAT)
    gram = jnp.dot(doc_grads, doc_grads.T, precision=lax.Precision.HIGHEST)
    damp = 0.1 * jnp.trace(gram) / NDOCS
    cross = jnp.dot(doc_grads, test_grads.astype(jnp.float32).T, precision=lax.Precision.HIGHEST)
    matrix = gram / NDOCS + damp * jnp.eye(NDOCS, dtype=jnp.float32)
    factor = jnp.linalg.cholesky(matrix)
    middle = lax.linalg.triangular_solve(factor, cross, left_side=True, lower=True)
    solved = lax.linalg.triangular_solve(factor, middle, left_side=True, lower=True, transpose_a=True)
    placing = (doc_ids[None, :] == jnp.arange(NDOCS, dtype=jnp.int32)[:, None]).astype(jnp.float32)
    return jnp.dot(placing, solved, precision=lax.Precision.HIGHEST)
```

```python
import jax
import jax.numpy as jnp
from jax import lax
from jax.experimental import pallas as pl
from jax.experimental.pallas import tpu as pltpu
from jax.sharding import PartitionSpec as P

MESH = pl.DeviceIdType.MESH
F32 = jnp.float32
BF16 = jnp.bfloat16
HIGH = lax.Precision.HIGHEST
NX, NY, NZ = 4, 8, 8
NSEQ, NDP = NX * NY, 2 * NZ
KO, KP, KI = 448, 512, 128
NDOCS = 64
NT = (((1,), (1,)), ((), ()))
Y_ORDER = (1, 7, 2, 6, 3, 5, 4)
X_ORDER = (1, 3, 2)


def kernel(
    in_hbm, og_hbm, valid_ref, blocks_ref, pin_ref, pout_ref, test_ref, out_ref,
    tok, grad, wo, wi, pad, send_b, recv_b, send_c, recv_c, recv_c2, send_d, recv_d, send_e, recv_e,
    load_sem, so, si, sdo, sdi, ro, ri, rso, rsi, rgo, rgi, phase_send, phase_recv,
):
    dp = lax.axis_index("dp")
    seq = lax.axis_index("seq")
    core = lax.rem(dp, 2)
    sibling = (dp + 1 - 2 * core, seq)
    x, y = seq // NY, lax.rem(seq, NY)

    def shard(i, j):
        return lax.rem(x + i, NX) * NY + lax.rem(y + j, NY)

    load_tok = pltpu.make_async_copy(in_hbm, tok, load_sem.at[0])
    load_grad = pltpu.make_async_copy(og_hbm, grad, load_sem.at[1])
    load_tok.start()
    load_grad.start()

    barrier = pltpu.get_barrier_semaphore()

    def greet_seq(i, carry):
        pl.semaphore_signal(
            barrier, inc=1, device_id=(dp, lax.rem(seq + i, NSEQ)), device_id_type=MESH
        )
        return carry

    def greet_dp(i, carry):
        pl.semaphore_signal(
            barrier, inc=1, device_id=(lax.rem(dp + i, NDP), seq), device_id_type=MESH
        )
        return carry

    lax.fori_loop(1, NSEQ, greet_seq, 0)
    lax.fori_loop(1, NDP, greet_dp, 0)

    row = lax.broadcasted_iota(jnp.int32, (64, 64), 0)
    col = lax.broadcasted_iota(jnp.int32, (64, 64), 1)
    source = jnp.where(row < 32, 2 * row, 2 * row - 63)
    order = jnp.where(col == source, 1.0, 0.0).astype(BF16)
    pad[...] = jnp.zeros_like(pad)
    pad[:, 0:KO] = jnp.dot(order, pout_ref[...], preferred_element_type=F32)
    left = pad[...]
    right = pltpu.roll(left, KP - KO, 1)
    odd = lax.rem(seq, 2)
    own_out = jnp.where(odd == 1, right, left).astype(BF16)
    wo[seq, 0] = own_out[0:32]
    wo[seq, 1] = own_out[32:64]
    wi[seq, 0] = pin_ref[0:32, :]
    wi[seq, 1] = pin_ref[32:64, :]

    pl.semaphore_wait(barrier, NSEQ - 1 + NDP - 1)

    def send_out(k, i, j):
        pltpu.make_async_remote_copy(
            wo.at[k, core], wo.at[k, core], so, ro.at[k],
            device_id=(dp, shard(i, j)), device_id_type=MESH,
        ).start()

    def send_in(k, i, j):
        pltpu.make_async_remote_copy(
            wi.at[k, core], wi.at[k, core], si, ri.at[k],
            device_id=(dp, shard(i, j)), device_id_type=MESH,
        ).start()

    def recv_out(k):
        pltpu.make_async_remote_copy(
            wo.at[k, core], wo.at[k, core], so, ro.at[k], device_id=sibling, device_id_type=MESH
        ).wait_recv()

    def recv_in(k):
        pltpu.make_async_remote_copy(
            wi.at[k, core], wi.at[k, core], si, ri.at[k], device_id=sibling, device_id_type=MESH
        ).wait_recv()

    for i in X_ORDER:
        send_in(seq, i, 0)
    for j in Y_ORDER:
        send_out(seq, 0, j)
    for i in X_ORDER:
        send_out(seq, i, 0)
    for j in Y_ORDER:
        send_in(seq, 0, j)

    def forward_in(i):
        k = shard(i, 0)
        recv_in(k)
        for j in Y_ORDER:
            send_in(k, 0, j)

    def forward_out(j):
        k = shard(0, j)
        recv_out(k)
        for i in X_ORDER:
            send_out(k, i, 0)
        pltpu.make_async_remote_copy(
            wo.at[k, core], wo.at[k, core], sdo, rso.at[k], device_id=sibling, device_id_type=MESH
        ).start()

    forward_in(1)
    forward_in(3)
    forward_out(1)
    forward_out(7)
    forward_in(2)
    for j in (2, 6, 3, 5, 4):
        forward_out(j)

    for j in Y_ORDER:
        k = shard(0, j)
        recv_in(k)
        pltpu.make_async_remote_copy(
            wi.at[k, core], wi.at[k, core], sdi, rsi.at[k], device_id=sibling, device_id_type=MESH
        ).start()

    load_tok.wait()
    load_grad.wait()

    def product(group):
        first = pl.multiple_of(group * NY, NY)
        lane = lax.broadcasted_iota(jnp.int32, (64, 128), 1)
        parts = []
        for q in range(NY // 2):
            even = wo[first + 2 * q].reshape(64, KP)
            odds = wo[first + 2 * q + 1].reshape(64, KP)
            joint = jnp.where(lane < 64, even[:, 384:512].astype(F32), odds[:, 0:128].astype(F32))
            parts += [even[:, 0:384], joint.astype(BF16), odds[:, 128:512]]
        weights = jnp.concatenate(parts, axis=1)
        columns = pl.ds(pl.multiple_of(group * NY * KO, NY * KO), NY * KO)
        pg = lax.dot_general(weights, grad[:, columns], NT, preferred_element_type=F32)
        weights = jnp.concatenate([wi[first + q].reshape(64, KI) for q in range(NY)], axis=1)
        columns = pl.ds(pl.multiple_of(group * NY * KI, NY * KI), NY * KI)
        px = lax.dot_general(weights, tok[:, columns], NT, preferred_element_type=F32)
        return pg, px

    def gather_sibling_row():
        for j in Y_ORDER:
            k = shard(0, j)
            pltpu.make_async_remote_copy(
                wo.at[k, core], wo.at[k, 1 - core], sdo, rso.at[k],
                device_id=sibling, device_id_type=MESH,
            ).wait_recv()
            pltpu.make_async_remote_copy(
                wi.at[k, core], wi.at[k, 1 - core], sdi, rsi.at[k],
                device_id=sibling, device_id_type=MESH,
            ).wait_recv()

    def exchange_group(i):
        group = lax.rem(x + i, NX)
        for j in (0,) + Y_ORDER:
            recv_out(shard(i, j))
        for j in Y_ORDER:
            recv_in(shard(i, j))
        rows = pl.ds(pl.multiple_of(group * NY, NY), NY)
        pltpu.make_async_remote_copy(
            wo.at[rows, core], wo.at[rows, core], sdo, rgo.at[i - 1],
            device_id=sibling, device_id_type=MESH,
        ).start()
        pltpu.make_async_remote_copy(
            wi.at[rows, core], wi.at[rows, core], sdi, rgi.at[i - 1],
            device_id=sibling, device_id_type=MESH,
        ).start()

    def await_group(i):
        group = lax.rem(x + i, NX)
        rows = pl.ds(pl.multiple_of(group * NY, NY), NY)
        pltpu.make_async_remote_copy(
            wo.at[rows, core], wo.at[rows, 1 - core], sdo, rgo.at[i - 1],
            device_id=sibling, device_id_type=MESH,
        ).wait_recv()
        pltpu.make_async_remote_copy(
            wi.at[rows, core], wi.at[rows, 1 - core], sdi, rgi.at[i - 1],
            device_id=sibling, device_id_type=MESH,
        ).wait_recv()
        return group

    gather_sibling_row()
    pg, px = product(x)
    exchange_group(1)
    exchange_group(3)
    more_g, more_x = product(await_group(1))
    pg, px = pg + more_g, px + more_x
    more_g, more_x = product(await_group(3))
    pg, px = pg + more_g, px + more_x
    exchange_group(2)
    more_g, more_x = product(await_group(2))
    pg, px = pg + more_g, px + more_x

    pg = jnp.where(valid_ref[...] == 1, pg, 0.0)
    block_grad = lax.dot_general(pg, px, NT, precision=HIGH, preferred_element_type=F32)
    folded = jnp.concatenate([block_grad[0:32], block_grad[32:64]], axis=1)
    send_b[...] = folded.reshape(NSEQ, 1, 128)

    def seq_copy(phase, src, dst, i):
        return pltpu.make_async_remote_copy(
            src, dst, phase_send.at[phase], phase_recv.at[phase],
            device_id=(dp, lax.rem(seq + i, NSEQ)), device_id_type=MESH,
        )

    def dp_copy(phase, src, dst, i):
        return pltpu.make_async_remote_copy(
            src, dst, phase_send.at[phase], phase_recv.at[phase],
            device_id=(lax.rem(dp + i, NDP), seq), device_id_type=MESH,
        )

    def scatter(i, carry):
        seq_copy(0, send_b.at[lax.rem(seq + i, NSEQ)], recv_b.at[seq], i).start()
        return carry

    lax.fori_loop(1, NSEQ, scatter, 0)
    recv_b[seq] = send_b[seq]
    block = lax.broadcasted_iota(jnp.int32, (8, NSEQ), 1)
    doc = lax.broadcasted_iota(jnp.int32, (8, NSEQ), 0)
    owner = jnp.zeros((8, NSEQ), jnp.int32)
    end = 0
    for j in range(4):
        end = end + blocks_ref[0, j]
        owner = owner + jnp.where(block >= end, 1, 0)
    member = jnp.where(owner == doc, 1.0, 0.0)
    seq_copy(0, recv_b.at[pl.ds(0, NSEQ - 1)], recv_b.at[pl.ds(0, NSEQ - 1)], 1).wait_recv()
    blocks = recv_b[...].reshape(NSEQ, 128)
    docs = jnp.dot(member, blocks, precision=HIGH, preferred_element_type=F32)
    send_c[...] = docs[0:4]

    def gather_dp(i, carry):
        dp_copy(1, send_c, recv_c.at[dp], i).start()
        return carry

    def gather_seq(i, carry):
        seq_copy(2, send_c, recv_c2.at[seq], i).start()
        return carry

    lax.fori_loop(1, NDP, gather_dp, 0)
    lax.fori_loop(1, NSEQ, gather_seq, 0)
    recv_c[dp] = docs[0:4]
    recv_c2[seq] = docs[0:4]

    dp_copy(1, recv_c.at[pl.ds(0, NDP - 1)], recv_c.at[pl.ds(0, NDP - 1)], 1).wait_recv()
    every = recv_c[...].reshape(NDOCS, 128)
    partial = lax.dot_general(docs, every, NT, precision=HIGH, preferred_element_type=F32)
    send_d[...] = partial[0:4]

    def reduce_seq(i, carry):
        seq_copy(3, send_d, recv_d.at[seq], i).start()
        return carry

    lax.fori_loop(1, NSEQ, reduce_seq, 0)
    recv_d[seq] = partial[0:4]

    seq_copy(2, recv_c2.at[pl.ds(0, NSEQ - 1)], recv_c2.at[pl.ds(0, NSEQ - 1)], 1).wait_recv()
    own = jnp.concatenate([recv_c2[t] for t in range(NSEQ)], axis=1)
    high = own.astype(BF16)
    rest = own - high.astype(F32)
    middle = rest.astype(BF16)
    low = (rest - middle.astype(F32)).astype(BF16)
    test = test_ref[...]
    cross = lax.dot_general(high, test, NT, preferred_element_type=F32)
    cross = cross + (
        lax.dot_general(middle, test, NT, preferred_element_type=F32)
        + lax.dot_general(low, test, NT, preferred_element_type=F32)
    )

    seq_copy(3, recv_d.at[pl.ds(0, NSEQ - 1)], recv_d.at[pl.ds(0, NSEQ - 1)], 1).wait_recv()
    gram_rows = jnp.sum(recv_d[...], axis=0)
    send_e[...] = jnp.zeros_like(send_e)
    send_e[:, 0:64] = gram_rows
    send_e[:, 64:96] = cross

    def gather_rows(i, carry):
        dp_copy(4, send_e, recv_e.at[dp], i).start()
        return carry

    lax.fori_loop(1, NDP, gather_rows, 0)
    recv_e[dp] = send_e[...]
    dp_copy(4, recv_e.at[pl.ds(0, NDP - 1)], recv_e.at[pl.ds(0, NDP - 1)], 1).wait_recv()
    out_ref[...] = recv_e[...].reshape(NDOCS, 128)

    for sem, buf in ((so, wo), (sdo, wo), (si, wi), (sdi, wi)):
        part = buf.at[pl.ds(0, NSEQ - 1), 0]
        pltpu.make_async_remote_copy(
            part, part, sem, ro.at[0], device_id=sibling, device_id_type=MESH
        ).wait_send()
    seq_copy(0, send_b.at[pl.ds(0, NSEQ - 1)], send_b.at[pl.ds(0, NSEQ - 1)], 1).wait_send()
    dp_copy(1, recv_c.at[pl.ds(0, NDP - 1)], recv_c.at[pl.ds(0, NDP - 1)], 1).wait_send()
    seq_copy(2, recv_c2.at[pl.ds(0, NSEQ - 1)], recv_c2.at[pl.ds(0, NSEQ - 1)], 1).wait_send()
    seq_copy(3, recv_d.at[pl.ds(0, NSEQ - 1)], recv_d.at[pl.ds(0, NSEQ - 1)], 1).wait_send()
    dp_copy(4, recv_e.at[pl.ds(0, NDP - 1)], recv_e.at[pl.ds(0, NDP - 1)], 1).wait_send()


def exchange(tokens, outgrad, valid, doc_blocks, proj_in, proj_out, test_grads):
    vmem = pl.BlockSpec(memory_space=pltpu.VMEM)
    anywhere = pl.BlockSpec(memory_space=pl.ANY)
    dma = pltpu.SemaphoreType.DMA
    return pl.pallas_call(
        kernel,
        name="attribution",
        out_shape=jax.ShapeDtypeStruct((NDOCS, 128), F32),
        in_specs=[
            anywhere, anywhere, vmem, pl.BlockSpec(memory_space=pltpu.SMEM), vmem, vmem, vmem,
        ],
        out_specs=vmem,
        scratch_shapes=[
            pltpu.VMEM((128, 4096), BF16),
            pltpu.VMEM((128, 14336), BF16),
            pltpu.VMEM((NSEQ, 2, 32, KP), BF16),
            pltpu.VMEM((NSEQ, 2, 32, KI), BF16),
            pltpu.VMEM((64, KP), F32),
            pltpu.VMEM((NSEQ, 1, 128), F32),
            pltpu.VMEM((NSEQ, 1, 128), F32),
            pltpu.VMEM((4, 128), F32),
            pltpu.VMEM((NDP, 4, 128), F32),
            pltpu.VMEM((NSEQ, 4, 128), F32),
            pltpu.VMEM((4, 64), F32),
            pltpu.VMEM((NSEQ, 4, 64), F32),
            pltpu.VMEM((4, 128), F32),
            pltpu.VMEM((NDP, 4, 128), F32),
            dma((2,)),
            dma, dma, dma, dma,
            dma((NSEQ,)), dma((NSEQ,)), dma((NSEQ,)), dma((NSEQ,)),
            dma((NX - 1,)), dma((NX - 1,)),
            dma((5,)), dma((5,)),
        ],
        compiler_params=pltpu.CompilerParams(
            collective_id=0, has_side_effects=True, vmem_limit_bytes=40 << 20
        ),
    )(tokens, outgrad, valid, doc_blocks, proj_in.T, proj_out.T, test_grads)


def per_device(inputs, out_grads, valid, doc_blocks, doc_ids, proj_in, proj_out, test_grads):
    both = exchange(inputs[0], out_grads[0], valid, doc_blocks, proj_in, proj_out, test_grads)
    gram, cross = both[:, 0:64], both[:, 64:96]
    damp = 0.1 * jnp.trace(gram) / NDOCS
    matrix = gram / NDOCS + damp * jnp.eye(NDOCS, dtype=F32)
    factor = jnp.linalg.cholesky(matrix)
    middle = lax.linalg.triangular_solve(factor, cross, left_side=True, lower=True)
    solved = lax.linalg.triangular_solve(
        factor, middle, left_side=True, lower=True, transpose_a=True
    )
    placing = (doc_ids[None, :] == jnp.arange(NDOCS, dtype=jnp.int32)[:, None]).astype(F32)
    return jnp.dot(placing, solved, precision=HIGH)


def solution(mesh):
    in_specs = (
        P("dp", "seq", None),
        P("dp", "seq", None),
        P("dp", "seq"),
        P("dp", None),
        P(),
        P("seq", None),
        P("seq", None),
        P("seq", None),
    )
    return jax.shard_map(
        per_device, mesh=mesh, in_specs=in_specs, out_specs=P(None, "seq"), check_vma=False
    )
```

```python
import jax
import jax.numpy as jnp
from jax import lax
from jax.experimental import pallas as pl
from jax.experimental.pallas import tpu as pltpu
from jax.sharding import PartitionSpec as P

MESH = pl.DeviceIdType.MESH
F32 = jnp.float32
BF16 = jnp.bfloat16
HIGH = lax.Precision.HIGHEST
NX, NY, NZ = 4, 8, 8
NSEQ, NDP = NX * NY, 2 * NZ
KO, KP, KI = 448, 512, 128
NDOCS = 64
NT = (((1,), (1,)), ((), ()))
Y_ORDER = (1, 7, 2, 6, 3, 5, 4)
X_ORDER = (1, 3, 2)


def inverse2(p, q, s):
    scale = 1.0 / (p * s - q * q)
    return s * scale, -q * scale, p * scale


def solve(both, ids):
    row = lax.broadcasted_iota(jnp.int32, (NDOCS, 128), 0)
    lane = lax.broadcasted_iota(jnp.int32, (NDOCS, 128), 1)
    diagonal = jnp.where(row == lane, both, 0.0)
    trace = jnp.sum(jnp.sum(diagonal, axis=0, keepdims=True), axis=1, keepdims=True)
    a = jnp.where(lane < NDOCS, both, NDOCS * both) / trace
    a = a + jnp.where(row == lane, 0.1, 0.0)
    for k in range(0, NDOCS, 4):
        r = [a[k + i : k + i + 1, :] for i in range(4)]
        c = [jnp.broadcast_to(a[:, k + i : k + i + 1], (NDOCS, 128)) for i in range(4)]
        m = [[c[j][k + i : k + i + 1] for j in range(4)] for i in range(4)]
        a00, a01, a11 = inverse2(m[0][0], m[1][0], m[1][1])
        b00, b01, b10, b11 = m[2][0], m[3][0], m[2][1], m[3][1]
        w00, w01 = a00 * b00 + a01 * b10, a00 * b01 + a01 * b11
        w10, w11 = a01 * b00 + a11 * b10, a01 * b01 + a11 * b11
        s00 = m[2][2] - (b00 * w00 + b10 * w10)
        s01 = m[3][2] - (b00 * w01 + b10 * w11)
        s11 = m[3][3] - (b01 * w01 + b11 * w11)
        e00, e01, e11 = inverse2(s00, s01, s11)
        t2 = r[2] - (w00 * r[0] + w10 * r[1])
        t3 = r[3] - (w01 * r[0] + w11 * r[1])
        u2, u3 = e00 * t2 + e01 * t3, e01 * t2 + e11 * t3
        u0 = a00 * r[0] + a01 * r[1] - (w00 * u2 + w01 * u3)
        u1 = a01 * r[0] + a11 * r[1] - (w10 * u2 + w11 * u3)
        rest = a - ((c[0] * u0 + c[1] * u1) + (c[2] * u2 + c[3] * u3))
        for i, u in enumerate((u0, u1, u2, u3)):
            rest = jnp.where(row == k + i, u, rest)
        a = rest
    number = lax.broadcasted_iota(jnp.int32, (NDOCS, NDOCS), 0)
    placing = jnp.where(ids == number, 1.0, 0.0)
    return jnp.dot(placing, a[:, 64:96], precision=HIGH, preferred_element_type=F32)


def kernel(
    in_hbm, og_hbm, valid_hbm, blocks_hbm, pin_hbm, pout_hbm, test_hbm, ids_hbm, out_ref,
    tok, grad, valid_ref, blocks_ref, pin_ref, pout_ref, test_ref, ids_ref, wo, wi, pad, send_b, recv_b, send_c, recv_c, recv_c2, send_d, recv_d, send_e, recv_e,
    load_sem, so, si, sdo, sdi, ro, ri, rso, rsi, rgo, rgi, phase_send, phase_recv,
):
    dp = lax.axis_index("dp")
    seq = lax.axis_index("seq")
    core = lax.rem(dp, 2)
    sibling = (dp + 1 - 2 * core, seq)
    x, y = seq // NY, lax.rem(seq, NY)

    def shard(i, j):
        return lax.rem(x + i, NX) * NY + lax.rem(y + j, NY)

    def load(i, src, dst):
        copy = pltpu.make_async_copy(src, dst, load_sem.at[i])
        copy.start()
        return copy

    load_pout = load(0, pout_hbm, pout_ref)
    load_pin = load(1, pin_hbm, pin_ref)
    later = [
        load(2, in_hbm, tok),
        load(3, og_hbm, grad),
        load(4, valid_hbm, valid_ref),
        load(5, blocks_hbm, blocks_ref),
        load(6, test_hbm, test_ref),
        load(7, ids_hbm, ids_ref),
    ]

    barrier = pltpu.get_barrier_semaphore()

    def greet_seq(i, carry):
        pl.semaphore_signal(
            barrier, inc=1, device_id=(dp, lax.rem(seq + i, NSEQ)), device_id_type=MESH
        )
        return carry

    def greet_dp(i, carry):
        pl.semaphore_signal(
            barrier, inc=1, device_id=(lax.rem(dp + i, NDP), seq), device_id_type=MESH
        )
        return carry

    lax.fori_loop(1, NSEQ, greet_seq, 0)
    lax.fori_loop(1, NDP, greet_dp, 0)

    def finish(last):
        for sem, buf in ((so, wo), (sdo, wo), (si, wi), (sdi, wi)):
            part = buf.at[pl.ds(0, NSEQ - 1), 0]
            pltpu.make_async_remote_copy(
                part, part, sem, ro.at[0], device_id=sibling, device_id_type=MESH
            ).wait_send()
        for phase, buf, count in (
            (0, send_b, NSEQ), (1, recv_c, NDP), (2, recv_c2, NSEQ), (3, recv_d, NSEQ), (4, recv_e, NDP),
        ):
            if phase <= last:
                part = buf.at[pl.ds(0, count - 1)]
                pltpu.make_async_remote_copy(
                    part, part, phase_send.at[phase], phase_recv.at[phase],
                    device_id=sibling, device_id_type=MESH,
                ).wait_send()

    row = lax.broadcasted_iota(jnp.int32, (64, 64), 0)
    col = lax.broadcasted_iota(jnp.int32, (64, 64), 1)
    source = jnp.where(row < 32, 2 * row, 2 * row - 63)
    order = jnp.where(col == source, 1.0, 0.0).astype(BF16)
    pad[...] = jnp.zeros_like(pad)
    load_pout.wait()
    load_pin.wait()
    pad[:, 0:KO] = jnp.dot(order, pout_ref[...], preferred_element_type=F32)
    left = pad[...]
    right = pltpu.roll(left, KP - KO, 1)
    odd = lax.rem(seq, 2)
    own_out = jnp.where(odd == 1, right, left).astype(BF16)
    wo[seq, 0] = own_out[0:32]
    wo[seq, 1] = own_out[32:64]
    wi[seq, 0] = pin_ref[0:32, :]
    wi[seq, 1] = pin_ref[32:64, :]

    pl.semaphore_wait(barrier, NSEQ - 1 + NDP - 1)

    def send_out(k, i, j):
        pltpu.make_async_remote_copy(
            wo.at[k, core], wo.at[k, core], so, ro.at[k],
            device_id=(dp, shard(i, j)), device_id_type=MESH,
        ).start()

    def send_in(k, i, j):
        pltpu.make_async_remote_copy(
            wi.at[k, core], wi.at[k, core], si, ri.at[k],
            device_id=(dp, shard(i, j)), device_id_type=MESH,
        ).start()

    def recv_out(k):
        pltpu.make_async_remote_copy(
            wo.at[k, core], wo.at[k, core], so, ro.at[k], device_id=sibling, device_id_type=MESH
        ).wait_recv()

    def recv_in(k):
        pltpu.make_async_remote_copy(
            wi.at[k, core], wi.at[k, core], si, ri.at[k], device_id=sibling, device_id_type=MESH
        ).wait_recv()

    for i in X_ORDER:
        send_in(seq, i, 0)
    for j in Y_ORDER:
        send_out(seq, 0, j)
    for i in X_ORDER:
        send_out(seq, i, 0)
    for j in Y_ORDER:
        send_in(seq, 0, j)

    def forward_in(i):
        k = shard(i, 0)
        recv_in(k)
        for j in Y_ORDER:
            send_in(k, 0, j)

    def forward_out(j):
        k = shard(0, j)
        recv_out(k)
        for i in X_ORDER:
            send_out(k, i, 0)
        pltpu.make_async_remote_copy(
            wo.at[k, core], wo.at[k, core], sdo, rso.at[k], device_id=sibling, device_id_type=MESH
        ).start()

    forward_in(1)
    forward_in(3)
    forward_out(1)
    forward_out(7)
    forward_in(2)
    for j in (2, 6, 3, 5, 4):
        forward_out(j)

    for j in Y_ORDER:
        k = shard(0, j)
        recv_in(k)
        pltpu.make_async_remote_copy(
            wi.at[k, core], wi.at[k, core], sdi, rsi.at[k], device_id=sibling, device_id_type=MESH
        ).start()

    for copy in later:
        copy.wait()

    def product(group):
        first = pl.multiple_of(group * NY, NY)
        lane = lax.broadcasted_iota(jnp.int32, (64, 128), 1)
        parts = []
        for q in range(NY // 2):
            even = wo[first + 2 * q].reshape(64, KP)
            odds = wo[first + 2 * q + 1].reshape(64, KP)
            joint = jnp.where(lane < 64, even[:, 384:512].astype(F32), odds[:, 0:128].astype(F32))
            parts += [even[:, 0:384], joint.astype(BF16), odds[:, 128:512]]
        weights = jnp.concatenate(parts, axis=1)
        columns = pl.ds(pl.multiple_of(group * NY * KO, NY * KO), NY * KO)
        pg = lax.dot_general(weights, grad[:, columns], NT, preferred_element_type=F32)
        weights = jnp.concatenate([wi[first + q].reshape(64, KI) for q in range(NY)], axis=1)
        columns = pl.ds(pl.multiple_of(group * NY * KI, NY * KI), NY * KI)
        px = lax.dot_general(weights, tok[:, columns], NT, preferred_element_type=F32)
        return pg, px

    def gather_sibling_row():
        for j in Y_ORDER:
            k = shard(0, j)
            pltpu.make_async_remote_copy(
                wo.at[k, core], wo.at[k, 1 - core], sdo, rso.at[k],
                device_id=sibling, device_id_type=MESH,
            ).wait_recv()
            pltpu.make_async_remote_copy(
                wi.at[k, core], wi.at[k, 1 - core], sdi, rsi.at[k],
                device_id=sibling, device_id_type=MESH,
            ).wait_recv()

    def exchange_group(i):
        group = lax.rem(x + i, NX)
        for j in (0,) + Y_ORDER:
            recv_out(shard(i, j))
        for j in Y_ORDER:
            recv_in(shard(i, j))
        rows = pl.ds(pl.multiple_of(group * NY, NY), NY)
        pltpu.make_async_remote_copy(
            wo.at[rows, core], wo.at[rows, core], sdo, rgo.at[i - 1],
            device_id=sibling, device_id_type=MESH,
        ).start()
        pltpu.make_async_remote_copy(
            wi.at[rows, core], wi.at[rows, core], sdi, rgi.at[i - 1],
            device_id=sibling, device_id_type=MESH,
        ).start()

    def await_group(i):
        group = lax.rem(x + i, NX)
        rows = pl.ds(pl.multiple_of(group * NY, NY), NY)
        pltpu.make_async_remote_copy(
            wo.at[rows, core], wo.at[rows, 1 - core], sdo, rgo.at[i - 1],
            device_id=sibling, device_id_type=MESH,
        ).wait_recv()
        pltpu.make_async_remote_copy(
            wi.at[rows, core], wi.at[rows, 1 - core], sdi, rgi.at[i - 1],
            device_id=sibling, device_id_type=MESH,
        ).wait_recv()
        return group

    gather_sibling_row()
    pg, px = product(x)
    exchange_group(1)
    exchange_group(3)
    more_g, more_x = product(await_group(1))
    pg, px = pg + more_g, px + more_x
    more_g, more_x = product(await_group(3))
    pg, px = pg + more_g, px + more_x
    exchange_group(2)
    more_g, more_x = product(await_group(2))
    pg, px = pg + more_g, px + more_x

    pg = jnp.where(valid_ref[...] == 1, pg, 0.0)
    block_grad = lax.dot_general(pg, px, NT, precision=HIGH, preferred_element_type=F32)
    folded = jnp.concatenate([block_grad[0:32], block_grad[32:64]], axis=1)
    send_b[...] = folded.reshape(NSEQ, 1, 128)

    def seq_copy(phase, src, dst, i):
        return pltpu.make_async_remote_copy(
            src, dst, phase_send.at[phase], phase_recv.at[phase],
            device_id=(dp, lax.rem(seq + i, NSEQ)), device_id_type=MESH,
        )

    def dp_copy(phase, src, dst, i):
        return pltpu.make_async_remote_copy(
            src, dst, phase_send.at[phase], phase_recv.at[phase],
            device_id=(lax.rem(dp + i, NDP), seq), device_id_type=MESH,
        )

    def scatter(i, carry):
        seq_copy(0, send_b.at[lax.rem(seq + i, NSEQ)], recv_b.at[seq], i).start()
        return carry

    lax.fori_loop(1, NSEQ, scatter, 0)
    recv_b[seq] = send_b[seq]
    block = lax.broadcasted_iota(jnp.int32, (8, NSEQ), 1)
    doc = lax.broadcasted_iota(jnp.int32, (8, NSEQ), 0)
    owner = jnp.zeros((8, NSEQ), jnp.int32)
    end = 0
    for j in range(4):
        end = end + blocks_ref[0, j]
        owner = owner + jnp.where(block >= end, 1, 0)
    member = jnp.where(owner == doc, 1.0, 0.0)
    seq_copy(0, recv_b.at[pl.ds(0, NSEQ - 1)], recv_b.at[pl.ds(0, NSEQ - 1)], 1).wait_recv()
    blocks = recv_b[...].reshape(NSEQ, 128)
    docs = jnp.dot(member, blocks, precision=HIGH, preferred_element_type=F32)
    send_c[...] = docs[0:4]

    def gather_dp(i, carry):
        dp_copy(1, send_c, recv_c.at[dp], i).start()
        return carry

    def gather_seq(i, carry):
        seq_copy(2, send_c, recv_c2.at[seq], i).start()
        return carry

    lax.fori_loop(1, NDP, gather_dp, 0)
    lax.fori_loop(1, NSEQ, gather_seq, 0)
    recv_c[dp] = docs[0:4]
    recv_c2[seq] = docs[0:4]

    dp_copy(1, recv_c.at[pl.ds(0, NDP - 1)], recv_c.at[pl.ds(0, NDP - 1)], 1).wait_recv()
    every = recv_c[...].reshape(NDOCS, 128)
    partial = lax.dot_general(docs, every, NT, precision=HIGH, preferred_element_type=F32)
    send_d[...] = partial[0:4]

    def reduce_seq(i, carry):
        seq_copy(3, send_d, recv_d.at[seq], i).start()
        return carry

    lax.fori_loop(1, NSEQ, reduce_seq, 0)
    recv_d[seq] = partial[0:4]

    seq_copy(2, recv_c2.at[pl.ds(0, NSEQ - 1)], recv_c2.at[pl.ds(0, NSEQ - 1)], 1).wait_recv()
    own = jnp.concatenate([recv_c2[t] for t in range(NSEQ)], axis=1)
    high = own.astype(BF16)
    rest = own - high.astype(F32)
    middle = rest.astype(BF16)
    low = (rest - middle.astype(F32)).astype(BF16)
    test = test_ref[...]
    cross = lax.dot_general(high, test, NT, preferred_element_type=F32)
    cross = cross + (
        lax.dot_general(middle, test, NT, preferred_element_type=F32)
        + lax.dot_general(low, test, NT, preferred_element_type=F32)
    )

    seq_copy(3, recv_d.at[pl.ds(0, NSEQ - 1)], recv_d.at[pl.ds(0, NSEQ - 1)], 1).wait_recv()
    gram_rows = jnp.sum(recv_d[...], axis=0)
    send_e[...] = jnp.zeros_like(send_e)
    send_e[:, 0:64] = gram_rows
    send_e[:, 64:96] = cross

    def gather_rows(i, carry):
        dp_copy(4, send_e, recv_e.at[dp], i).start()
        return carry

    lax.fori_loop(1, NDP, gather_rows, 0)
    recv_e[dp] = send_e[...]
    dp_copy(4, recv_e.at[pl.ds(0, NDP - 1)], recv_e.at[pl.ds(0, NDP - 1)], 1).wait_recv()
    out_ref[...] = solve(recv_e[...].reshape(NDOCS, 128), ids_ref[...])
    finish(4)


def exchange(tokens, outgrad, valid, doc_blocks, doc_ids, proj_in, proj_out, test_grads):
    vmem = pl.BlockSpec(memory_space=pltpu.VMEM)
    dma = pltpu.SemaphoreType.DMA
    return pl.pallas_call(
        kernel,
        name="attribution",
        out_shape=jax.ShapeDtypeStruct((NDOCS, 32), F32),
        in_specs=[pl.BlockSpec(memory_space=pltpu.HBM)] * 8,
        out_specs=vmem,
        scratch_shapes=[
            pltpu.VMEM((128, 4096), BF16),
            pltpu.VMEM((128, 14336), BF16),
            pltpu.VMEM((1, 128), jnp.int32),
            pltpu.SMEM((1, 4), jnp.int32),
            pltpu.VMEM((64, KI), BF16),
            pltpu.VMEM((64, KO), BF16),
            pltpu.VMEM((32, 4096), BF16),
            pltpu.VMEM((1, NDOCS), jnp.int32),
            pltpu.VMEM((NSEQ, 2, 32, KP), BF16),
            pltpu.VMEM((NSEQ, 2, 32, KI), BF16),
            pltpu.VMEM((64, KP), F32),
            pltpu.VMEM((NSEQ, 1, 128), F32),
            pltpu.VMEM((NSEQ, 1, 128), F32),
            pltpu.VMEM((4, 128), F32),
            pltpu.VMEM((NDP, 4, 128), F32),
            pltpu.VMEM((NSEQ, 4, 128), F32),
            pltpu.VMEM((4, 64), F32),
            pltpu.VMEM((NSEQ, 4, 64), F32),
            pltpu.VMEM((4, 128), F32),
            pltpu.VMEM((NDP, 4, 128), F32),
            dma((8,)),
            dma, dma, dma, dma,
            dma((NSEQ,)), dma((NSEQ,)), dma((NSEQ,)), dma((NSEQ,)),
            dma((NX - 1,)), dma((NX - 1,)),
            dma((5,)), dma((5,)),
        ],
        compiler_params=pltpu.CompilerParams(
            collective_id=0, has_side_effects=True, vmem_limit_bytes=60 << 20
        ),
    )(tokens, outgrad, valid, doc_blocks, proj_in.T, proj_out.T, test_grads, doc_ids.reshape(1, NDOCS))


def per_device(inputs, out_grads, valid, doc_blocks, doc_ids, proj_in, proj_out, test_grads):
    return exchange(
        inputs[0], out_grads[0], valid, doc_blocks, doc_ids, proj_in, proj_out, test_grads
    )


def solution(mesh):
    in_specs = (
        P("dp", "seq", None),
        P("dp", "seq", None),
        P("dp", "seq"),
        P("dp", None),
        P(),
        P("seq", None),
        P("seq", None),
        P("seq", None),
    )
    return jax.shard_map(
        per_device, mesh=mesh, in_specs=in_specs, out_specs=P(None, "seq"), check_vma=False
    )
```

```python
import jax
import jax.numpy as jnp
from jax import lax
from jax.experimental import pallas as pl
from jax.experimental.pallas import tpu as pltpu
from jax.sharding import PartitionSpec as P

MESH = pl.DeviceIdType.MESH
F32 = jnp.float32
BF16 = jnp.bfloat16
HIGH = lax.Precision.HIGHEST
NX, NY, NZ = 4, 8, 8
NSEQ, NDP = NX * NY, 2 * NZ
KO, KP, KI = 448, 512, 128
NDOCS = 64
NT = (((1,), (1,)), ((), ()))
Y_ORDER = (1, 7, 2, 6, 3, 5, 4)
X_ORDER = (1, 3, 2)


def reach(step, size):
    return min(step, size - step)


PLANE = sorted(
    [(i, j) for i in range(NX) for j in range(NY) if i or j],
    key=lambda o: -reach(o[0], NX) - reach(o[1], NY),
)
STACK = sorted(
    [(k, e) for k in range(NZ) for e in range(2) if k or e],
    key=lambda o: -2 * reach(o[0], NZ) - o[1],
)


def inverse2(p, q, s):
    scale = 1.0 / (p * s - q * q)
    return s * scale, -q * scale, p * scale


def solve(both, ids):
    row = lax.broadcasted_iota(jnp.int32, (NDOCS, 128), 0)
    lane = lax.broadcasted_iota(jnp.int32, (NDOCS, 128), 1)
    diagonal = jnp.where(row == lane, both, 0.0)
    trace = jnp.sum(jnp.sum(diagonal, axis=0, keepdims=True), axis=1, keepdims=True)
    a = jnp.where(lane < NDOCS, both, NDOCS * both) / trace
    a = a + jnp.where(row == lane, 0.1, 0.0)
    for k in range(0, NDOCS, 4):
        r = [a[k + i : k + i + 1, :] for i in range(4)]
        c = [jnp.broadcast_to(a[:, k + i : k + i + 1], (NDOCS, 128)) for i in range(4)]
        m = [[c[j][k + i : k + i + 1] for j in range(4)] for i in range(4)]
        a00, a01, a11 = inverse2(m[0][0], m[1][0], m[1][1])
        b00, b01, b10, b11 = m[2][0], m[3][0], m[2][1], m[3][1]
        w00, w01 = a00 * b00 + a01 * b10, a00 * b01 + a01 * b11
        w10, w11 = a01 * b00 + a11 * b10, a01 * b01 + a11 * b11
        s00 = m[2][2] - (b00 * w00 + b10 * w10)
        s01 = m[3][2] - (b00 * w01 + b10 * w11)
        s11 = m[3][3] - (b01 * w01 + b11 * w11)
        e00, e01, e11 = inverse2(s00, s01, s11)
        t2 = r[2] - (w00 * r[0] + w10 * r[1])
        t3 = r[3] - (w01 * r[0] + w11 * r[1])
        u2, u3 = e00 * t2 + e01 * t3, e01 * t2 + e11 * t3
        u0 = a00 * r[0] + a01 * r[1] - (w00 * u2 + w01 * u3)
        u1 = a01 * r[0] + a11 * r[1] - (w10 * u2 + w11 * u3)
        rest = a - ((c[0] * u0 + c[1] * u1) + (c[2] * u2 + c[3] * u3))
        for i, u in enumerate((u0, u1, u2, u3)):
            rest = jnp.where(row == k + i, u, rest)
        a = rest
    number = lax.broadcasted_iota(jnp.int32, (NDOCS, NDOCS), 0)
    placing = jnp.where(ids == number, 1.0, 0.0)
    return lax.dot_general(
        a[:, 64:96], placing, (((0,), (1,)), ((), ())), precision=HIGH, preferred_element_type=F32
    )


def kernel(
    in_hbm, og_hbm, valid_hbm, blocks_hbm, pin_hbm, pout_hbm, test_hbm, ids_hbm, out_ref,
    tok, grad, valid_ref, blocks_ref, pin_ref, pout_ref, test_ref, ids_ref, w2, w3, pad,
    send_b, recv_b, send_c, recv_c, recv_c2, send_d, recv_d, send_e, recv_e,
    load_sem, gather_send, r2, r2_sib, r3, r3_z, r3_sib, phase_send, phase_recv,
):
    dp = lax.axis_index("dp")
    seq = lax.axis_index("seq")
    z, core = dp // 2, lax.rem(dp, 2)
    x, y = seq // NY, lax.rem(seq, NY)

    def shard(i, j):
        return lax.rem(x + i, NX) * NY + lax.rem(y + j, NY)

    def level(k, e):
        return lax.rem(z + k, NZ) * 2 + (core + e * (1 - 2 * core))

    sibling = (level(0, 1), seq)

    def load(i, src, dst):
        copy = pltpu.make_async_copy(src, dst, load_sem.at[i])
        copy.start()
        return copy

    load_pout = load(0, pout_hbm, pout_ref)
    load_pin = load(1, pin_hbm, pin_ref)
    later = [
        load(2, in_hbm, tok),
        load(3, og_hbm, grad),
        load(4, valid_hbm, valid_ref),
        load(5, blocks_hbm, blocks_ref),
        load(6, test_hbm, test_ref),
        load(7, ids_hbm, ids_ref),
    ]

    barrier = pltpu.get_barrier_semaphore()
    for i, j in PLANE:
        pl.semaphore_signal(barrier, inc=1, device_id=(dp, shard(i, j)), device_id_type=MESH)
    for k, e in STACK:
        pl.semaphore_signal(barrier, inc=1, device_id=(level(k, e), seq), device_id_type=MESH)

    def remote(src, dst, send, recv, target):
        return pltpu.make_async_remote_copy(
            src, dst, send, recv, device_id=target, device_id_type=MESH
        )

    def finish(last):
        for sem, part in (
            (0, w2.at[pl.ds(0, NSEQ - 1), 0]),
            (1, w2.at[pl.ds(0, NSEQ - 1), 0]),
            (2, w3.at[0, 0, pl.ds(0, NSEQ - 1)]),
            (3, w3.at[0, pl.ds(0, 3)]),
            (4, w3.at[0]),
        ):
            remote(part, part, gather_send.at[sem], r2.at[0], sibling).wait_send()
        for phase, buf, count in (
            (0, send_b, NSEQ), (1, recv_c, NDP), (2, recv_c2, NSEQ), (3, recv_d, NSEQ), (4, recv_e, NDP),
        ):
            if phase <= last:
                part = buf.at[pl.ds(0, count - 1)]
                remote(
                    part, part, phase_send.at[phase], phase_recv.at[phase], sibling
                ).wait_send()

    row = lax.broadcasted_iota(jnp.int32, (64, 64), 0)
    col = lax.broadcasted_iota(jnp.int32, (64, 64), 1)
    source = jnp.where(row < 32, 2 * row, 2 * row - 63)
    order = jnp.where(col == source, 1.0, 0.0).astype(BF16)
    pad[...] = jnp.zeros_like(pad)
    load_pout.wait()
    load_pin.wait()
    pad[:, 0:KO] = jnp.dot(order, pout_ref[...], preferred_element_type=F32)
    left = pad[...]
    right = pltpu.roll(left, KP - KO, 1)
    own_out = jnp.where(lax.rem(seq, 2) == 1, right, left).astype(BF16)
    pad[...] = own_out.astype(F32)
    for half in range(2):
        rows = slice(32 * half, 32 * half + 32)
        w2[seq, half, :, 0:256] = own_out[rows, 256:512]
        w2[seq, half, :, 256:384] = pin_ref[rows, :]
    part = lax.rem(z, 4)
    quarter = pad[pl.ds(pl.multiple_of(part * 16, 16), 16), 0:256]
    w3[core, part, seq] = jnp.where(core == 1, quarter[:, 128:256], quarter[:, 0:128]).astype(BF16)

    pl.semaphore_wait(barrier, NSEQ - 1 + NDP - 1)

    def send_2(k, i, j):
        piece = w2.at[k, core]
        remote(piece, piece, gather_send.at[0], r2.at[k], (dp, shard(i, j))).start()

    def recv_2(k):
        piece = w2.at[k, core]
        remote(piece, piece, gather_send.at[0], r2.at[k], sibling).wait_recv()
        remote(piece, piece, gather_send.at[1], r2_sib.at[k], sibling).start()

    def group_of(i):
        return lax.rem(x + i, NX)

    def bundle(tile, quarter_index, group):
        return w3.at[tile, quarter_index, pl.ds(pl.multiple_of(group * NY, NY), NY)]

    def share(group, quarter_index):
        piece = bundle(core, quarter_index, group)
        sem = r3_sib.at[group * 4 + quarter_index]
        remote(piece, piece, gather_send.at[4], sem, sibling).start()

    steps = (1, NZ - 1, 2)

    def lift(i):
        group = group_of(i)
        for j in Y_ORDER + ((0,) if i else ()):
            piece = w3.at[core, part, shard(i, j)]
            remote(piece, piece, gather_send.at[2], r3.at[shard(i, j)], sibling).wait_recv()
        piece = bundle(core, part, group)
        for e, step in enumerate(steps):
            far = step if e < 2 else 2 + 4 * core
            target = (lax.rem(z + far, NZ) * 2 + core, seq)
            sem = r3_z.at[group * 3 + e]
            remote(piece, piece, gather_send.at[3], sem, target).start()
        share(group, part)

    def land(i):
        group = group_of(i)
        for e, step in enumerate(steps):
            far = step if e < 2 else 2 + 4 * core
            origin = lax.rem(z + NZ - far, 4)
            piece = bundle(core, origin, group)
            sem = r3_z.at[group * 3 + e]
            remote(piece, piece, gather_send.at[3], sem, sibling).wait_recv()
            share(group, origin)

    def settle(i):
        group = group_of(i)
        for j in range(NY):
            if i or j:
                k = shard(i, j)
                piece = w2.at[k, 1 - core]
                remote(piece, piece, gather_send.at[1], r2_sib.at[k], sibling).wait_recv()
        for q in range(4):
            piece = bundle(1 - core, q, group)
            sem = r3_sib.at[group * 4 + q]
            remote(piece, piece, gather_send.at[4], sem, sibling).wait_recv()

    for j in Y_ORDER:
        send_2(seq, 0, j)
    for i in X_ORDER:
        send_2(seq, i, 0)
    for i in (0,) + X_ORDER:
        for j in (4, 5, 3, 6, 2, 7, 1) + ((0,) if i else ()):
            piece = w3.at[core, part, seq]
            remote(piece, piece, gather_send.at[2], r3.at[seq], (dp, shard(i, j))).start()

    def pass_on(j):
        k = shard(0, j)
        recv_2(k)
        for i in X_ORDER:
            send_2(k, i, 0)

    def collect(i):
        for j in (0,) + Y_ORDER:
            recv_2(shard(i, j))

    def product(group):
        first = pl.multiple_of(group * NY, NY)
        lane = lax.broadcasted_iota(jnp.int32, (64, 128), 1)
        parts = []
        for q in range(0, NY, 2):
            even, odds = w2[first + q].reshape(64, 384), w2[first + q + 1].reshape(64, 384)
            odd_0 = w3[0, :, first + q + 1].reshape(64, 128)
            joint = jnp.where(lane < 64, even[:, 128:256].astype(F32), odd_0.astype(F32))
            parts += [
                w3[0, :, first + q].reshape(64, 128),
                w3[1, :, first + q].reshape(64, 128),
                even[:, 0:128],
                joint.astype(BF16),
                w3[1, :, first + q + 1].reshape(64, 128),
                odds[:, 0:256],
            ]
        weights = jnp.concatenate(parts, axis=1)
        columns = pl.ds(pl.multiple_of(group * NY * KO, NY * KO), NY * KO)
        pg = lax.dot_general(weights, grad[:, columns], NT, preferred_element_type=F32)
        weights = jnp.concatenate(
            [w2[first + q].reshape(64, 384)[:, 256:384] for q in range(NY)], axis=1
        )
        columns = pl.ds(pl.multiple_of(group * NY * KI, NY * KI), NY * KI)
        px = lax.dot_general(weights, tok[:, columns], NT, preferred_element_type=F32)
        return pg, px

    for j in (1, 7, 2, 6):
        pass_on(j)
    lift(0)
    for j in (3, 5, 4):
        pass_on(j)
    lift(1)
    lift(3)
    for copy in later:
        copy.wait()
    land(0)
    lift(2)
    settle(0)
    pg, px = product(x)
    collect(1)
    land(1)
    collect(3)
    land(3)
    settle(1)
    more_g, more_x = product(group_of(1))
    pg, px = pg + more_g, px + more_x
    settle(3)
    more_g, more_x = product(group_of(3))
    pg, px = pg + more_g, px + more_x
    collect(2)
    land(2)
    settle(2)
    more_g, more_x = product(group_of(2))
    pg, px = pg + more_g, px + more_x

    pg = jnp.where(valid_ref[...] == 1, pg, 0.0)
    block_grad = lax.dot_general(pg, px, NT, precision=HIGH, preferred_element_type=F32)
    folded = jnp.concatenate([block_grad[0:32], block_grad[32:64]], axis=1)
    send_b[...] = folded.reshape(NSEQ, 1, 128)

    def plane_send(phase, src, dst):
        for i, j in PLANE:
            target = (dp, shard(i, j))
            remote(src(shard(i, j)), dst, phase_send.at[phase], phase_recv.at[phase], target).start()

    def stack_send(phase, src, dst):
        for k, e in STACK:
            target = (level(k, e), seq)
            remote(src, dst, phase_send.at[phase], phase_recv.at[phase], target).start()

    def await_all(phase, buf, count):
        part = buf.at[pl.ds(0, count - 1)]
        remote(part, part, phase_send.at[phase], phase_recv.at[phase], sibling).wait_recv()

    plane_send(0, lambda peer: send_b.at[peer], recv_b.at[seq])
    recv_b[seq] = send_b[seq]
    block = lax.broadcasted_iota(jnp.int32, (8, NSEQ), 1)
    doc = lax.broadcasted_iota(jnp.int32, (8, NSEQ), 0)
    owner = jnp.zeros((8, NSEQ), jnp.int32)
    end = 0
    for j in range(4):
        end = end + blocks_ref[0, j]
        owner = owner + jnp.where(block >= end, 1, 0)
    member = jnp.where(owner == doc, 1.0, 0.0)
    await_all(0, recv_b, NSEQ)
    blocks = recv_b[...].reshape(NSEQ, 128)
    docs = jnp.dot(member, blocks, precision=HIGH, preferred_element_type=F32)
    send_c[...] = docs[0:4]
    stack_send(1, send_c, recv_c.at[dp])
    plane_send(2, lambda peer: send_c, recv_c2.at[seq])
    recv_c[dp] = docs[0:4]
    recv_c2[seq] = docs[0:4]

    await_all(1, recv_c, NDP)
    every = recv_c[...].reshape(NDOCS, 128)
    partial = lax.dot_general(docs, every, NT, precision=HIGH, preferred_element_type=F32)
    send_d[...] = partial[0:4]
    plane_send(3, lambda peer: send_d, recv_d.at[seq])
    recv_d[seq] = partial[0:4]

    await_all(2, recv_c2, NSEQ)
    own = jnp.concatenate([recv_c2[t] for t in range(NSEQ)], axis=1)
    high = own.astype(BF16)
    rest = own - high.astype(F32)
    middle = rest.astype(BF16)
    low = (rest - middle.astype(F32)).astype(BF16)
    test = test_ref[...]
    cross = lax.dot_general(high, test, NT, preferred_element_type=F32)
    cross = cross + (
        lax.dot_general(middle, test, NT, preferred_element_type=F32)
        + lax.dot_general(low, test, NT, preferred_element_type=F32)
    )
    send_e[...] = jnp.zeros_like(send_e)
    send_e[:, 64:96] = cross

    await_all(3, recv_d, NSEQ)
    send_e[:, 0:64] = jnp.sum(recv_d[...], axis=0)
    stack_send(4, send_e, recv_e.at[dp])
    recv_e[dp] = send_e[...]
    await_all(4, recv_e, NDP)
    out_ref[...] = solve(recv_e[...].reshape(NDOCS, 128), ids_ref[...])
    finish(4)


def exchange(tokens, outgrad, valid, doc_blocks, doc_ids, proj_in, proj_out, test_grads):
    vmem = pl.BlockSpec(memory_space=pltpu.VMEM)
    dma = pltpu.SemaphoreType.DMA
    return pl.pallas_call(
        kernel,
        name="attribution",
        out_shape=jax.ShapeDtypeStruct((32, NDOCS), F32),
        in_specs=[pl.BlockSpec(memory_space=pltpu.HBM)] * 8,
        out_specs=vmem,
        scratch_shapes=[
            pltpu.VMEM((128, 4096), BF16),
            pltpu.VMEM((128, 14336), BF16),
            pltpu.VMEM((1, 128), jnp.int32),
            pltpu.SMEM((1, 4), jnp.int32),
            pltpu.VMEM((64, KI), BF16),
            pltpu.VMEM((64, KO), BF16),
            pltpu.VMEM((32, 4096), BF16),
            pltpu.VMEM((1, NDOCS), jnp.int32),
            pltpu.VMEM((NSEQ, 2, 32, 384), BF16),
            pltpu.VMEM((2, 4, NSEQ, 16, 128), BF16),
            pltpu.VMEM((64, KP), F32),
            pltpu.VMEM((NSEQ, 1, 128), F32),
            pltpu.VMEM((NSEQ, 1, 128), F32),
            pltpu.VMEM((4, 128), F32),
            pltpu.VMEM((NDP, 4, 128), F32),
            pltpu.VMEM((NSEQ, 4, 128), F32),
            pltpu.VMEM((4, 64), F32),
            pltpu.VMEM((NSEQ, 4, 64), F32),
            pltpu.VMEM((4, 128), F32),
            pltpu.VMEM((NDP, 4, 128), F32),
            dma((8,)),
            dma((5,)),
            dma((NSEQ,)), dma((NSEQ,)), dma((NSEQ,)),
            dma((NX * 3,)), dma((NX * 4,)),
            dma((5,)), dma((5,)),
        ],
        compiler_params=pltpu.CompilerParams(
            collective_id=0, has_side_effects=True, vmem_limit_bytes=60 << 20
        ),
    )(tokens, outgrad, valid, doc_blocks, proj_in.T, proj_out.T, test_grads, doc_ids.reshape(1, NDOCS)).T


def per_device(inputs, out_grads, valid, doc_blocks, doc_ids, proj_in, proj_out, test_grads):
    return exchange(
        inputs[0], out_grads[0], valid, doc_blocks, doc_ids, proj_in, proj_out, test_grads
    )


def solution(mesh):
    in_specs = (
        P("dp", "seq", None),
        P("dp", "seq", None),
        P("dp", "seq"),
        P("dp", None),
        P(),
        P("seq", None),
        P("seq", None),
        P("seq", None),
    )
    return jax.shard_map(
        per_device, mesh=mesh, in_specs=in_specs, out_specs=P(None, "seq"), check_vma=False
    )
```

```python
import jax
import jax.numpy as jnp
from jax import lax
from jax.experimental import pallas as pl
from jax.experimental.pallas import tpu as pltpu
from jax.sharding import PartitionSpec as P

MESH = pl.DeviceIdType.MESH
F32 = jnp.float32
BF16 = jnp.bfloat16
HIGH = lax.Precision.HIGHEST
NX, NY, NZ = 4, 8, 8
NSEQ, NDP = NX * NY, 2 * NZ
KO, KP, KI = 448, 512, 128
NDOCS = 64
NT = (((1,), (1,)), ((), ()))
Y_ORDER = (1, 7, 2, 6, 3, 5, 4)
X_ORDER = (1, 3, 2)


def reach(step, size):
    return min(step, size - step)


PLANE = sorted(
    [(i, j) for i in range(NX) for j in range(NY) if i or j],
    key=lambda o: -reach(o[0], NX) - reach(o[1], NY),
)
STACK = sorted(
    [(k, e) for k in range(NZ) for e in range(2) if k or e],
    key=lambda o: -2 * reach(o[0], NZ) - o[1],
)


def inverse2(p, q, s):
    scale = 1.0 / (p * s - q * q)
    return s * scale, -q * scale, p * scale


def solve(both):
    row = lax.broadcasted_iota(jnp.int32, (NDOCS, 128), 0)
    lane = lax.broadcasted_iota(jnp.int32, (NDOCS, 128), 1)
    diagonal = jnp.where(row == lane, both, 0.0)
    trace = jnp.sum(jnp.sum(diagonal, axis=0, keepdims=True), axis=1, keepdims=True)
    a = jnp.where(lane < NDOCS, both, NDOCS * both) / trace
    a = a + jnp.where(row == lane, 0.1, 0.0)
    for k in range(0, NDOCS, 4):
        r = [a[k + i : k + i + 1, :] for i in range(4)]
        c = [jnp.broadcast_to(a[:, k + i : k + i + 1], (NDOCS, 128)) for i in range(4)]
        m = [[c[j][k + i : k + i + 1] for j in range(4)] for i in range(4)]
        a00, a01, a11 = inverse2(m[0][0], m[1][0], m[1][1])
        b00, b01, b10, b11 = m[2][0], m[3][0], m[2][1], m[3][1]
        w00, w01 = a00 * b00 + a01 * b10, a00 * b01 + a01 * b11
        w10, w11 = a01 * b00 + a11 * b10, a01 * b01 + a11 * b11
        s00 = m[2][2] - (b00 * w00 + b10 * w10)
        s01 = m[3][2] - (b00 * w01 + b10 * w11)
        s11 = m[3][3] - (b01 * w01 + b11 * w11)
        e00, e01, e11 = inverse2(s00, s01, s11)
        t2 = r[2] - (w00 * r[0] + w10 * r[1])
        t3 = r[3] - (w01 * r[0] + w11 * r[1])
        u2, u3 = e00 * t2 + e01 * t3, e01 * t2 + e11 * t3
        u0 = a00 * r[0] + a01 * r[1] - (w00 * u2 + w01 * u3)
        u1 = a01 * r[0] + a11 * r[1] - (w10 * u2 + w11 * u3)
        rest = a - ((c[0] * u0 + c[1] * u1) + (c[2] * u2 + c[3] * u3))
        for i, u in enumerate((u0, u1, u2, u3)):
            rest = jnp.where(row == k + i, u, rest)
        a = rest
    return a[:, 64:96]


def kernel(
    in_hbm, og_hbm, valid_hbm, blocks_hbm, pin_hbm, pout_hbm, test_hbm, out_ref,
    tok, grad, valid_ref, blocks_ref, pin_ref, pout_ref, test_ref, w2, w3, pad,
    send_b, recv_b, send_c, recv_c, recv_c2, send_d, recv_d, send_e, recv_e,
    load_sem, gather_send, r2, r2_sib, r3, r3_z, r3_sib, phase_send, phase_recv,
):
    dp = lax.axis_index("dp")
    seq = lax.axis_index("seq")
    z, core = dp // 2, lax.rem(dp, 2)
    x, y = seq // NY, lax.rem(seq, NY)

    def shard(i, j):
        return lax.rem(x + i, NX) * NY + lax.rem(y + j, NY)

    def level(k, e):
        return lax.rem(z + k, NZ) * 2 + (core + e * (1 - 2 * core))

    sibling = (level(0, 1), seq)

    def load(i, src, dst):
        copy = pltpu.make_async_copy(src, dst, load_sem.at[i])
        copy.start()
        return copy

    load_pout = load(0, pout_hbm, pout_ref)
    load_pin = load(1, pin_hbm, pin_ref)
    later = [
        load(2, in_hbm, tok),
        load(3, og_hbm, grad),
        load(4, valid_hbm, valid_ref),
        load(5, blocks_hbm, blocks_ref),
        load(6, test_hbm, test_ref),
    ]

    barrier = pltpu.get_barrier_semaphore()
    for i, j in PLANE:
        pl.semaphore_signal(barrier, inc=1, device_id=(dp, shard(i, j)), device_id_type=MESH)
    for k, e in STACK:
        pl.semaphore_signal(barrier, inc=1, device_id=(level(k, e), seq), device_id_type=MESH)

    def remote(src, dst, send, recv, target):
        return pltpu.make_async_remote_copy(
            src, dst, send, recv, device_id=target, device_id_type=MESH
        )

    def finish(last):
        for sem, part in (
            (0, w2.at[pl.ds(0, NSEQ - 1), 0]),
            (1, w2.at[pl.ds(0, NSEQ - 1), 0]),
            (2, w3.at[0, 0, pl.ds(0, NSEQ - 1)]),
            (3, w3.at[0, pl.ds(0, 3)]),
            (4, w3.at[0]),
        ):
            remote(part, part, gather_send.at[sem], r2.at[0], sibling).wait_send()
        for phase, buf, count in (
            (0, send_b, NSEQ), (1, recv_c, NDP), (2, recv_c2, NSEQ), (3, recv_d, NSEQ), (4, recv_e, NDP),
        ):
            if phase <= last:
                part = buf.at[pl.ds(0, count - 1)]
                remote(
                    part, part, phase_send.at[phase], phase_recv.at[phase], sibling
                ).wait_send()

    row = lax.broadcasted_iota(jnp.int32, (64, 64), 0)
    col = lax.broadcasted_iota(jnp.int32, (64, 64), 1)
    source = jnp.where(row < 32, 2 * row, 2 * row - 63)
    order = jnp.where(col == source, 1.0, 0.0).astype(BF16)
    pad[...] = jnp.zeros_like(pad)
    load_pout.wait()
    load_pin.wait()
    pad[:, 0:KO] = jnp.dot(order, pout_ref[...], preferred_element_type=F32)
    even_form = pad[...]
    own_out = jnp.where(lax.rem(seq, 2) == 1, pltpu.roll(even_form, KO, 1), even_form)
    pad[...] = own_out
    last = own_out[:, 384:512]
    last = last + pltpu.roll(last, 64, 1)
    lane = lax.broadcasted_iota(jnp.int32, (32, 128), 1)
    folded = jnp.where(lane < 64, last[0:32], last[32:64]).astype(BF16)
    for half in range(2):
        rows = slice(32 * half, 32 * half + 32)
        w2[seq, half, 0:2] = own_out[rows, 256:384].astype(BF16).reshape(2, 16, 128)
        w2[seq, half, 2:4] = pin_ref[rows, :].reshape(2, 16, 128)
        w2[seq, half, 4] = folded[16 * half : 16 * half + 16]
    part = lax.rem(z, 4)
    quarter = pad[pl.ds(pl.multiple_of(part * 16, 16), 16), 0:256]
    w3[core, part, seq] = jnp.where(core == 1, quarter[:, 128:256], quarter[:, 0:128]).astype(BF16)

    pl.semaphore_wait(barrier, NSEQ - 1 + NDP - 1)

    def send_2(k, i, j):
        piece = w2.at[k, core]
        remote(piece, piece, gather_send.at[0], r2.at[k], (dp, shard(i, j))).start()

    def recv_2(k):
        piece = w2.at[k, core]
        remote(piece, piece, gather_send.at[0], r2.at[k], sibling).wait_recv()
        remote(piece, piece, gather_send.at[1], r2_sib.at[k], sibling).start()

    def group_of(i):
        return lax.rem(x + i, NX)

    def bundle(tile, quarter_index, group):
        return w3.at[tile, quarter_index, pl.ds(pl.multiple_of(group * NY, NY), NY)]

    def share(group, quarter_index):
        piece = bundle(core, quarter_index, group)
        sem = r3_sib.at[group * 4 + quarter_index]
        remote(piece, piece, gather_send.at[4], sem, sibling).start()

    steps = (1, NZ - 1, 2)

    def lift(i):
        group = group_of(i)
        for j in Y_ORDER + ((0,) if i else ()):
            piece = w3.at[core, part, shard(i, j)]
            remote(piece, piece, gather_send.at[2], r3.at[shard(i, j)], sibling).wait_recv()
        piece = bundle(core, part, group)
        for e, step in enumerate(steps):
            far = step if e < 2 else 2 + 4 * core
            target = (lax.rem(z + far, NZ) * 2 + core, seq)
            sem = r3_z.at[group * 3 + e]
            remote(piece, piece, gather_send.at[3], sem, target).start()
        share(group, part)

    def land(i):
        group = group_of(i)
        for e, step in enumerate(steps):
            far = step if e < 2 else 2 + 4 * core
            origin = lax.rem(z + NZ - far, 4)
            piece = bundle(core, origin, group)
            sem = r3_z.at[group * 3 + e]
            remote(piece, piece, gather_send.at[3], sem, sibling).wait_recv()
            share(group, origin)

    def settle(i):
        group = group_of(i)
        for j in range(NY):
            if i or j:
                k = shard(i, j)
                piece = w2.at[k, 1 - core]
                remote(piece, piece, gather_send.at[1], r2_sib.at[k], sibling).wait_recv()
        for q in range(4):
            piece = bundle(1 - core, q, group)
            sem = r3_sib.at[group * 4 + q]
            remote(piece, piece, gather_send.at[4], sem, sibling).wait_recv()

    for i in (0,) + X_ORDER:
        for j in (4, 5, 3, 6, 2, 7, 1) + ((0,) if i else ()):
            piece = w3.at[core, part, seq]
            remote(piece, piece, gather_send.at[2], r3.at[seq], (dp, shard(i, j))).start()
    for j in Y_ORDER:
        send_2(seq, 0, j)
    for i in X_ORDER:
        send_2(seq, i, 0)

    def pass_on(j):
        k = shard(0, j)
        recv_2(k)
        for i in X_ORDER:
            send_2(k, i, 0)

    def collect(i):
        for j in (0,) + Y_ORDER:
            recv_2(shard(i, j))

    def product(group):
        first = pl.multiple_of(group * NY, NY)

        def tiles(k):
            three = [w3[0, :, k], w3[1, :, k], w2[k, :, 0:2]]
            return [t.reshape(64, 128) for t in three], w2[k, :, 4].reshape(32, 128).astype(F32)

        parts = []
        for q in range(0, NY, 2):
            (even, last_even), (odd, last_odd) = tiles(first + q), tiles(first + q + 1)
            upper = jnp.where(lane < 64, last_even, pltpu.roll(last_odd, 64, 1))
            lower = jnp.where(lane < 64, pltpu.roll(last_even, 64, 1), last_odd)
            joint = jnp.concatenate([upper, lower], axis=0).astype(BF16)
            parts += even + [joint] + odd
        weights = jnp.concatenate(parts, axis=1)
        columns = pl.ds(pl.multiple_of(group * NY * KO, NY * KO), NY * KO)
        pg = lax.dot_general(weights, grad[:, columns], NT, preferred_element_type=F32)
        weights = jnp.concatenate(
            [w2[first + q, :, 2:4].reshape(64, 128) for q in range(NY)], axis=1
        )
        columns = pl.ds(pl.multiple_of(group * NY * KI, NY * KI), NY * KI)
        px = lax.dot_general(weights, tok[:, columns], NT, preferred_element_type=F32)
        return pg, px

    lift(0)
    pass_on(1)
    pass_on(7)
    lift(1)
    lift(3)
    pass_on(2)
    pass_on(6)
    lift(2)
    land(0)
    pass_on(3)
    pass_on(5)
    land(1)
    pass_on(4)
    land(3)
    land(2)
    for copy in later:
        copy.wait()
    settle(0)
    pg, px = product(x)
    collect(1)
    collect(3)
    collect(2)
    for i in X_ORDER:
        settle(i)
        more_g, more_x = product(group_of(i))
        pg, px = pg + more_g, px + more_x

    pg = jnp.where(valid_ref[...] == 1, pg, 0.0)
    block_grad = lax.dot_general(pg, px, NT, precision=HIGH, preferred_element_type=F32)
    folded = jnp.concatenate([block_grad[0:32], block_grad[32:64]], axis=1)
    send_b[...] = folded.reshape(NSEQ, 1, 128)

    def plane_send(phase, src, dst):
        for i, j in PLANE:
            target = (dp, shard(i, j))
            remote(src(shard(i, j)), dst, phase_send.at[phase], phase_recv.at[phase], target).start()

    def stack_send(phase, src, dst):
        for k, e in STACK:
            target = (level(k, e), seq)
            remote(src, dst, phase_send.at[phase], phase_recv.at[phase], target).start()

    def await_all(phase, buf, count):
        part = buf.at[pl.ds(0, count - 1)]
        remote(part, part, phase_send.at[phase], phase_recv.at[phase], sibling).wait_recv()

    plane_send(0, lambda peer: send_b.at[peer], recv_b.at[seq])
    recv_b[seq] = send_b[seq]
    block = lax.broadcasted_iota(jnp.int32, (8, NSEQ), 1)
    doc = lax.broadcasted_iota(jnp.int32, (8, NSEQ), 0)
    owner = jnp.zeros((8, NSEQ), jnp.int32)
    end = 0
    for j in range(4):
        end = end + blocks_ref[0, j]
        owner = owner + jnp.where(block >= end, 1, 0)
    member = jnp.where(owner == doc, 1.0, 0.0)
    await_all(0, recv_b, NSEQ)
    blocks = recv_b[...].reshape(NSEQ, 128)
    docs = jnp.dot(member, blocks, precision=HIGH, preferred_element_type=F32)
    send_c[...] = docs[0:4]
    stack_send(1, send_c, recv_c.at[dp])
    plane_send(2, lambda peer: send_c, recv_c2.at[seq])
    recv_c[dp] = docs[0:4]
    recv_c2[seq] = docs[0:4]

    await_all(1, recv_c, NDP)
    every = recv_c[...].reshape(NDOCS, 128)
    partial = lax.dot_general(docs, every, NT, precision=HIGH, preferred_element_type=F32)
    send_d[...] = partial[0:4]
    plane_send(3, lambda peer: send_d, recv_d.at[seq])
    recv_d[seq] = partial[0:4]

    await_all(2, recv_c2, NSEQ)
    own = jnp.concatenate([recv_c2[t] for t in range(NSEQ)], axis=1)
    high = own.astype(BF16)
    rest = own - high.astype(F32)
    middle = rest.astype(BF16)
    low = (rest - middle.astype(F32)).astype(BF16)
    test = test_ref[...]
    cross = lax.dot_general(high, test, NT, preferred_element_type=F32)
    cross = cross + (
        lax.dot_general(middle, test, NT, preferred_element_type=F32)
        + lax.dot_general(low, test, NT, preferred_element_type=F32)
    )
    send_e[...] = jnp.zeros_like(send_e)
    send_e[:, 64:96] = cross

    await_all(3, recv_d, NSEQ)
    send_e[:, 0:64] = jnp.sum(recv_d[...], axis=0)
    stack_send(4, send_e, recv_e.at[dp])
    recv_e[dp] = send_e[...]
    await_all(4, recv_e, NDP)
    out_ref[...] = solve(recv_e[...].reshape(NDOCS, 128))
    finish(4)


def exchange(tokens, outgrad, valid, doc_blocks, proj_in, proj_out, test_grads):
    vmem = pl.BlockSpec(memory_space=pltpu.VMEM)
    dma = pltpu.SemaphoreType.DMA
    return pl.pallas_call(
        kernel,
        name="attribution",
        out_shape=jax.ShapeDtypeStruct((NDOCS, 32), F32),
        in_specs=[pl.BlockSpec(memory_space=pltpu.HBM)] * 7,
        out_specs=vmem,
        scratch_shapes=[
            pltpu.VMEM((128, 4096), BF16),
            pltpu.VMEM((128, 14336), BF16),
            pltpu.VMEM((1, 128), jnp.int32),
            pltpu.SMEM((1, 4), jnp.int32),
            pltpu.VMEM((64, KI), BF16),
            pltpu.VMEM((64, KO), BF16),
            pltpu.VMEM((32, 4096), BF16),
            pltpu.VMEM((NSEQ, 2, 5, 16, 128), BF16),
            pltpu.VMEM((2, 4, NSEQ, 16, 128), BF16),
            pltpu.VMEM((64, KP), F32),
            pltpu.VMEM((NSEQ, 1, 128), F32),
            pltpu.VMEM((NSEQ, 1, 128), F32),
            pltpu.VMEM((4, 128), F32),
            pltpu.VMEM((NDP, 4, 128), F32),
            pltpu.VMEM((NSEQ, 4, 128), F32),
            pltpu.VMEM((4, 64), F32),
            pltpu.VMEM((NSEQ, 4, 64), F32),
            pltpu.VMEM((4, 128), F32),
            pltpu.VMEM((NDP, 4, 128), F32),
            dma((7,)),
            dma((5,)),
            dma((NSEQ,)), dma((NSEQ,)), dma((NSEQ,)),
            dma((NX * 3,)), dma((NX * 4,)),
            dma((5,)), dma((5,)),
        ],
        compiler_params=pltpu.CompilerParams(
            collective_id=0, has_side_effects=True, vmem_limit_bytes=60 << 20
        ),
    )(tokens, outgrad, valid, doc_blocks, proj_in.T, proj_out.T, test_grads)


def per_device(inputs, out_grads, valid, doc_blocks, doc_ids, proj_in, proj_out, test_grads):
    solved = exchange(inputs[0], out_grads[0], valid, doc_blocks, proj_in, proj_out, test_grads)
    placing = (doc_ids[None, :] == jnp.arange(NDOCS, dtype=jnp.int32)[:, None]).astype(F32)
    return jnp.dot(placing, solved, precision=HIGH)


def solution(mesh):
    in_specs = (
        P("dp", "seq", None),
        P("dp", "seq", None),
        P("dp", "seq"),
        P("dp", None),
        P(),
        P("seq", None),
        P("seq", None),
        P("seq", None),
    )
    return jax.shard_map(
        per_device, mesh=mesh, in_specs=in_specs, out_specs=P(None, "seq"), check_vma=False
    )
```

```python
import jax
import jax.numpy as jnp
from jax import lax
from jax.experimental import pallas as pl
from jax.experimental.pallas import tpu as pltpu
from jax.sharding import PartitionSpec as P

MESH = pl.DeviceIdType.MESH
F32 = jnp.float32
BF16 = jnp.bfloat16
HIGH = lax.Precision.HIGHEST
NX, NY, NZ = 4, 8, 8
NSEQ, NDP = NX * NY, 2 * NZ
KO, KP, KI = 448, 512, 128
NDOCS = 64
NT = (((1,), (1,)), ((), ()))
Y_ORDER = (1, 7, 2, 6, 3, 5, 4)
X_ORDER = (1, 3, 2)


def reach(step, size):
    return min(step, size - step)


PLANE = sorted(
    [(i, j) for i in range(NX) for j in range(NY) if i or j],
    key=lambda o: -reach(o[0], NX) - reach(o[1], NY),
)
STACK = sorted(
    [(k, e) for k in range(NZ) for e in range(2) if k or e],
    key=lambda o: -2 * reach(o[0], NZ) - o[1],
)


def inverse2(p, q, s):
    scale = 1.0 / (p * s - q * q)
    return s * scale, -q * scale, p * scale


def solve(both, ids):
    row = lax.broadcasted_iota(jnp.int32, (NDOCS, 128), 0)
    lane = lax.broadcasted_iota(jnp.int32, (NDOCS, 128), 1)
    diagonal = jnp.where(row == lane, both, 0.0)
    trace = jnp.sum(jnp.sum(diagonal, axis=0, keepdims=True), axis=1, keepdims=True)
    a = both / trace + jnp.where(row == lane, 0.1, 0.0)
    for k in range(0, NDOCS, 4):
        r = [a[k + i : k + i + 1, :] for i in range(4)]
        c = [jnp.broadcast_to(a[:, k + i : k + i + 1], (NDOCS, 128)) for i in range(4)]
        m = [[c[j][k + i : k + i + 1] for j in range(4)] for i in range(4)]
        a00, a01, a11 = inverse2(m[0][0], m[1][0], m[1][1])
        b00, b01, b10, b11 = m[2][0], m[3][0], m[2][1], m[3][1]
        w00, w01 = a00 * b00 + a01 * b10, a00 * b01 + a01 * b11
        w10, w11 = a01 * b00 + a11 * b10, a01 * b01 + a11 * b11
        s00 = m[2][2] - (b00 * w00 + b10 * w10)
        s01 = m[3][2] - (b00 * w01 + b10 * w11)
        s11 = m[3][3] - (b01 * w01 + b11 * w11)
        e00, e01, e11 = inverse2(s00, s01, s11)
        t2 = r[2] - (w00 * r[0] + w10 * r[1])
        t3 = r[3] - (w01 * r[0] + w11 * r[1])
        u2, u3 = e00 * t2 + e01 * t3, e01 * t2 + e11 * t3
        u0 = a00 * r[0] + a01 * r[1] - (w00 * u2 + w01 * u3)
        u1 = a01 * r[0] + a11 * r[1] - (w10 * u2 + w11 * u3)
        rest = a - ((c[0] * u0 + c[1] * u1) + (c[2] * u2 + c[3] * u3))
        for i, u in enumerate((u0, u1, u2, u3)):
            rest = jnp.where(row == k + i, u, rest)
        a = rest
    number = lax.broadcasted_iota(jnp.int32, (NDOCS, NDOCS), 0)
    placing = jnp.where(ids == number, 1.0, 0.0)
    return lax.dot_general(
        a[:, 64:96], placing, (((0,), (1,)), ((), ())), precision=HIGH, preferred_element_type=F32
    )


def kernel(
    in_hbm, og_hbm, valid_hbm, blocks_hbm, pin_hbm, pout_hbm, test_hbm, ids_hbm, out_ref,
    tok, grad, valid_ref, blocks_ref, pin_ref, pout_ref, test_ref, ids_ref, w2, w3, pad,
    send_b, recv_b, send_c, recv_c, recv_c2, send_d, recv_d, send_e, recv_e, send_f, recv_f,
    load_sem, gather_send, r2, r2_sib, r3, r3_z, r3_sib, phase_send, phase_recv,
):
    dp = lax.axis_index("dp")
    seq = lax.axis_index("seq")
    z, core = dp // 2, lax.rem(dp, 2)
    x, y = seq // NY, lax.rem(seq, NY)

    def shard(i, j):
        return lax.rem(x + i, NX) * NY + lax.rem(y + j, NY)

    def level(k, e):
        return lax.rem(z + k, NZ) * 2 + (core + e * (1 - 2 * core))

    sibling = (level(0, 1), seq)

    def load(i, src, dst):
        copy = pltpu.make_async_copy(src, dst, load_sem.at[i])
        copy.start()
        return copy

    load_pout = load(0, pout_hbm, pout_ref)
    load_pin = load(1, pin_hbm, pin_ref)
    later = [
        load(2, in_hbm, tok),
        load(3, og_hbm, grad),
        load(4, valid_hbm, valid_ref),
        load(5, blocks_hbm, blocks_ref),
        load(6, test_hbm, test_ref),
        load(7, ids_hbm, ids_ref),
    ]

    barrier = pltpu.get_barrier_semaphore()
    for i, j in PLANE:
        pl.semaphore_signal(barrier, inc=1, device_id=(dp, shard(i, j)), device_id_type=MESH)
    for k, e in STACK:
        pl.semaphore_signal(barrier, inc=1, device_id=(level(k, e), seq), device_id_type=MESH)

    def remote(src, dst, send, recv, target):
        return pltpu.make_async_remote_copy(
            src, dst, send, recv, device_id=target, device_id_type=MESH
        )

    def finish(last):
        for sem, part in (
            (0, w2.at[pl.ds(0, NSEQ - 1), 0]),
            (1, w2.at[pl.ds(0, NSEQ - 1), 0]),
            (2, w3.at[0, 0, pl.ds(0, NSEQ - 1)]),
            (3, w3.at[0, pl.ds(0, 3)]),
            (4, w3.at[0]),
        ):
            remote(part, part, gather_send.at[sem], r2.at[0], sibling).wait_send()
        for phase, buf, count in (
            (0, send_b, NSEQ), (1, recv_c, NDP), (2, recv_c2, NSEQ), (3, recv_d, NSEQ), (4, recv_e, 8),
            (5, recv_f, NDP),
        ):
            if phase <= last:
                part = buf.at[pl.ds(0, count - 1)]
                remote(
                    part, part, phase_send.at[phase], phase_recv.at[phase], sibling
                ).wait_send()

    row = lax.broadcasted_iota(jnp.int32, (64, 64), 0)
    col = lax.broadcasted_iota(jnp.int32, (64, 64), 1)
    source = jnp.where(row < 32, 2 * row, 2 * row - 63)
    order = jnp.where(col == source, 1.0, 0.0).astype(BF16)
    pad[...] = jnp.zeros_like(pad)
    load_pout.wait()
    load_pin.wait()
    pad[:, 0:KO] = jnp.dot(order, pout_ref[...], preferred_element_type=F32)
    even_form = pad[...]
    own_out = jnp.where(lax.rem(seq, 2) == 1, pltpu.roll(even_form, KO, 1), even_form)
    pad[...] = own_out
    last = own_out[:, 384:512]
    last = last + pltpu.roll(last, 64, 1)
    lane = lax.broadcasted_iota(jnp.int32, (32, 128), 1)
    folded = jnp.where(lane < 64, last[0:32], last[32:64]).astype(BF16)
    for half in range(2):
        rows = slice(32 * half, 32 * half + 32)
        w2[seq, half, 0:2] = own_out[rows, 256:384].astype(BF16).reshape(2, 16, 128)
        w2[seq, half, 2:4] = pin_ref[rows, :].reshape(2, 16, 128)
        w2[seq, half, 4] = folded[16 * half : 16 * half + 16]
    part = lax.rem(z, 4)
    quarter = pad[pl.ds(pl.multiple_of(part * 16, 16), 16), 0:256]
    w3[core, part, seq] = jnp.where(core == 1, quarter[:, 128:256], quarter[:, 0:128]).astype(BF16)

    pl.semaphore_wait(barrier, NSEQ - 1 + NDP - 1)

    def send_2(k, i, j):
        piece = w2.at[k, core]
        remote(piece, piece, gather_send.at[0], r2.at[k], (dp, shard(i, j))).start()

    def recv_2(k):
        piece = w2.at[k, core]
        remote(piece, piece, gather_send.at[0], r2.at[k], sibling).wait_recv()
        remote(piece, piece, gather_send.at[1], r2_sib.at[k], sibling).start()

    def group_of(i):
        return lax.rem(x + i, NX)

    def bundle(tile, quarter_index, group):
        return w3.at[tile, quarter_index, pl.ds(pl.multiple_of(group * NY, NY), NY)]

    def share(group, quarter_index):
        piece = bundle(core, quarter_index, group)
        sem = r3_sib.at[group * 4 + quarter_index]
        remote(piece, piece, gather_send.at[4], sem, sibling).start()

    steps = (1, NZ - 1, 2)

    def lift(i):
        group = group_of(i)
        for j in Y_ORDER + ((0,) if i else ()):
            piece = w3.at[core, part, shard(i, j)]
            remote(piece, piece, gather_send.at[2], r3.at[shard(i, j)], sibling).wait_recv()
        piece = bundle(core, part, group)
        for e, step in enumerate(steps):
            far = step if e < 2 else 2 + 4 * core
            target = (lax.rem(z + far, NZ) * 2 + core, seq)
            sem = r3_z.at[group * 3 + e]
            remote(piece, piece, gather_send.at[3], sem, target).start()
        share(group, part)

    def land(i):
        group = group_of(i)
        for e, step in enumerate(steps):
            far = step if e < 2 else 2 + 4 * core
            origin = lax.rem(z + NZ - far, 4)
            piece = bundle(core, origin, group)
            sem = r3_z.at[group * 3 + e]
            remote(piece, piece, gather_send.at[3], sem, sibling).wait_recv()
            share(group, origin)

    def settle(i):
        group = group_of(i)
        for j in range(NY):
            if i or j:
                k = shard(i, j)
                piece = w2.at[k, 1 - core]
                remote(piece, piece, gather_send.at[1], r2_sib.at[k], sibling).wait_recv()
        for q in range(4):
            piece = bundle(1 - core, q, group)
            sem = r3_sib.at[group * 4 + q]
            remote(piece, piece, gather_send.at[4], sem, sibling).wait_recv()

    for i in (0,) + X_ORDER:
        for j in (4, 5, 3, 6, 2, 7, 1) + ((0,) if i else ()):
            piece = w3.at[core, part, seq]
            remote(piece, piece, gather_send.at[2], r3.at[seq], (dp, shard(i, j))).start()
    for i in X_ORDER:
        send_2(seq, i, 0)
    for j in Y_ORDER:
        send_2(seq, 0, j)

    def pass_on(j):
        k = shard(0, j)
        recv_2(k)
        for i in X_ORDER:
            send_2(k, i, 0)

    def collect(i):
        for j in (0,) + Y_ORDER:
            recv_2(shard(i, j))

    def product(group):
        first = pl.multiple_of(group * NY, NY)

        def tiles(k):
            three = [w3[0, :, k], w3[1, :, k], w2[k, :, 0:2]]
            return [t.reshape(64, 128) for t in three], w2[k, :, 4].reshape(32, 128).astype(F32)

        parts = []
        for q in range(0, NY, 2):
            (even, last_even), (odd, last_odd) = tiles(first + q), tiles(first + q + 1)
            upper = jnp.where(lane < 64, last_even, pltpu.roll(last_odd, 64, 1))
            lower = jnp.where(lane < 64, pltpu.roll(last_even, 64, 1), last_odd)
            joint = jnp.concatenate([upper, lower], axis=0).astype(BF16)
            parts += even + [joint] + odd
        weights = jnp.concatenate(parts, axis=1)
        columns = pl.ds(pl.multiple_of(group * NY * KO, NY * KO), NY * KO)
        pg = lax.dot_general(weights, grad[:, columns], NT, preferred_element_type=F32)
        weights = jnp.concatenate(
            [w2[first + q, :, 2:4].reshape(64, 128) for q in range(NY)], axis=1
        )
        columns = pl.ds(pl.multiple_of(group * NY * KI, NY * KI), NY * KI)
        px = lax.dot_general(weights, tok[:, columns], NT, preferred_element_type=F32)
        return pg, px

    lift(0)
    pass_on(1)
    pass_on(7)
    lift(1)
    lift(3)
    pass_on(2)
    pass_on(6)
    lift(2)
    pass_on(3)
    pass_on(5)
    pass_on(4)
    land(0)
    land(1)
    land(3)
    land(2)
    for copy in later:
        copy.wait()
    settle(0)
    pg, px = product(x)
    def add(i):
        more_g, more_x = product(group_of(i))
        return pg + more_g, px + more_x

    collect(1)
    collect(3)
    settle(1)
    pg, px = add(1)
    collect(2)
    settle(3)
    pg, px = add(3)
    settle(2)
    pg, px = add(2)

    pg = jnp.where(valid_ref[...] == 1, pg, 0.0)
    block_grad = lax.dot_general(pg, px, NT, precision=HIGH, preferred_element_type=F32)
    folded = jnp.concatenate([block_grad[0:32], block_grad[32:64]], axis=1)
    send_b[...] = folded.reshape(NSEQ, 1, 128)

    def plane_send(phase, src, dst):
        for i, j in PLANE:
            target = (dp, shard(i, j))
            remote(src(shard(i, j)), dst, phase_send.at[phase], phase_recv.at[phase], target).start()

    def stack_send(phase, src, dst):
        for k, e in STACK:
            target = (level(k, e), seq)
            remote(src, dst, phase_send.at[phase], phase_recv.at[phase], target).start()

    def await_all(phase, buf, count):
        part = buf.at[pl.ds(0, count - 1)]
        remote(part, part, phase_send.at[phase], phase_recv.at[phase], sibling).wait_recv()

    plane_send(0, lambda peer: send_b.at[peer], recv_b.at[seq])
    recv_b[seq] = send_b[seq]
    block = lax.broadcasted_iota(jnp.int32, (NSEQ, 128), 0)
    owner = jnp.zeros((NSEQ, 128), jnp.int32)
    end = 0
    for j in range(4):
        end = end + blocks_ref[0, j]
        owner = owner + jnp.where(block >= end, 1, 0)
    await_all(0, recv_b, NSEQ)
    blocks = recv_b[...].reshape(NSEQ, 128)
    for j in range(4):
        send_c[j : j + 1] = jnp.sum(jnp.where(owner == j, blocks, 0.0), axis=0, keepdims=True)
    stack_send(1, send_c, recv_c.at[dp])
    plane_send(2, lambda peer: send_c, recv_c2.at[seq])
    recv_c[dp] = send_c[...]
    recv_c2[seq] = send_c[...]

    await_all(1, recv_c, NDP)
    every = recv_c[...].reshape(NDOCS, 128)
    eighth = part * 2 + core
    mine = recv_c[pl.ds(eighth * 2, 2)].reshape(8, 128)
    partial = lax.dot_general(mine, every, NT, precision=HIGH, preferred_element_type=F32)
    send_d[...] = jnp.concatenate([partial[0:4], partial[4:8]], axis=1)
    plane_send(3, lambda peer: send_d, recv_d.at[seq])
    recv_d[seq] = send_d[...]

    await_all(2, recv_c2, NSEQ)
    own = jnp.concatenate([recv_c2[t] for t in range(NSEQ)], axis=1)
    high = own.astype(BF16)
    rest = own - high.astype(F32)
    middle = rest.astype(BF16)
    low = (rest - middle.astype(F32)).astype(BF16)
    test = test_ref[...]
    cross = lax.dot_general(high, test, NT, preferred_element_type=F32)
    cross = cross + (
        lax.dot_general(middle, test, NT, preferred_element_type=F32)
        + lax.dot_general(low, test, NT, preferred_element_type=F32)
    )
    send_f[...] = jnp.zeros_like(send_f)
    send_f[:, 64:96] = cross
    stack_send(5, send_f, recv_f.at[dp])
    recv_f[dp] = send_f[...]

    await_all(3, recv_d, NSEQ)
    send_e[...] = jnp.sum(recv_d[...], axis=0)
    for e, step in enumerate(steps):
        far = step if e < 2 else 2 + 4 * core
        for other in range(2):
            target = (lax.rem(z + far, NZ) * 2 + other, seq)
            remote(send_e, recv_e.at[eighth], phase_send.at[4], phase_recv.at[4], target).start()
    remote(send_e, recv_e.at[eighth], phase_send.at[4], phase_recv.at[4], sibling).start()
    recv_e[eighth] = send_e[...]
    await_all(5, recv_f, NDP)
    await_all(4, recv_e, 8)
    gram = recv_e[...]
    gram = jnp.concatenate([gram, pltpu.roll(gram, 64, 2)], axis=1).reshape(NDOCS, 128)
    lane = lax.broadcasted_iota(jnp.int32, (NDOCS, 128), 1)
    both = jnp.where(lane < NDOCS, gram, recv_f[...].reshape(NDOCS, 128))
    out_ref[...] = solve(both, ids_ref[...])
    finish(5)


def exchange(tokens, outgrad, valid, doc_blocks, doc_ids, proj_in, proj_out, test_grads):
    vmem = pl.BlockSpec(memory_space=pltpu.VMEM)
    dma = pltpu.SemaphoreType.DMA
    return pl.pallas_call(
        kernel,
        name="attribution",
        out_shape=jax.ShapeDtypeStruct((32, NDOCS), F32),
        in_specs=[pl.BlockSpec(memory_space=pltpu.HBM)] * 8,
        out_specs=vmem,
        scratch_shapes=[
            pltpu.VMEM((128, 4096), BF16),
            pltpu.VMEM((128, 14336), BF16),
            pltpu.VMEM((1, 128), jnp.int32),
            pltpu.SMEM((1, 4), jnp.int32),
            pltpu.VMEM((64, KI), BF16),
            pltpu.VMEM((64, KO), BF16),
            pltpu.VMEM((32, 4096), BF16),
            pltpu.VMEM((1, NDOCS), jnp.int32),
            pltpu.VMEM((NSEQ, 2, 5, 16, 128), BF16),
            pltpu.VMEM((2, 4, NSEQ, 16, 128), BF16),
            pltpu.VMEM((64, KP), F32),
            pltpu.VMEM((NSEQ, 1, 128), F32),
            pltpu.VMEM((NSEQ, 1, 128), F32),
            pltpu.VMEM((4, 128), F32),
            pltpu.VMEM((NDP, 4, 128), F32),
            pltpu.VMEM((NSEQ, 4, 128), F32),
            pltpu.VMEM((4, 128), F32),
            pltpu.VMEM((NSEQ, 4, 128), F32),
            pltpu.VMEM((4, 128), F32),
            pltpu.VMEM((8, 4, 128), F32),
            pltpu.VMEM((4, 128), F32),
            pltpu.VMEM((NDP, 4, 128), F32),
            dma((8,)),
            dma((5,)),
            dma((NSEQ,)), dma((NSEQ,)), dma((NSEQ,)),
            dma((NX * 3,)), dma((NX * 4,)),
            dma((6,)), dma((6,)),
        ],
        compiler_params=pltpu.CompilerParams(
            collective_id=0, has_side_effects=True, vmem_limit_bytes=60 << 20
        ),
    )(tokens, outgrad, valid, doc_blocks, proj_in.T, proj_out.T, test_grads, doc_ids.reshape(1, NDOCS))


def per_device(inputs, out_grads, valid, doc_blocks, doc_ids, proj_in, proj_out, test_grads):
    scaled = exchange(
        inputs[0], out_grads[0], valid, doc_blocks, doc_ids, proj_in, proj_out, test_grads
    )
    return NDOCS * scaled.T


def solution(mesh):
    in_specs = (
        P("dp", "seq", None),
        P("dp", "seq", None),
        P("dp", "seq"),
        P("dp", None),
        P(),
        P("seq", None),
        P("seq", None),
        P("seq", None),
    )
    return jax.shard_map(
        per_device, mesh=mesh, in_specs=in_specs, out_specs=P(None, "seq"), check_vma=False
    )
```

```python
import jax
import jax.numpy as jnp
from jax import lax
from jax.experimental import pallas as pl
from jax.experimental.pallas import tpu as pltpu
from jax.sharding import PartitionSpec as P

MESH = pl.DeviceIdType.MESH
F32 = jnp.float32
BF16 = jnp.bfloat16
HIGH = lax.Precision.HIGHEST
NX, NY, NZ = 4, 8, 8
NSEQ, NDP = NX * NY, 2 * NZ
KO, KP, KI = 448, 512, 128
NDOCS = 64
NT = (((1,), (1,)), ((), ()))
Y_ORDER = (1, 7, 2, 6, 3, 5, 4)
X_ORDER = (1, 3, 2)


def reach(step, size):
    return min(step, size - step)


PLANE = sorted(
    [(i, j) for i in range(NX) for j in range(NY) if i or j],
    key=lambda o: -reach(o[0], NX) - reach(o[1], NY),
)
STACK = sorted(
    [(k, e) for k in range(NZ) for e in range(2) if k or e],
    key=lambda o: -2 * reach(o[0], NZ) - o[1],
)


def adjugate4(m):
    s0 = m[0][0] * m[1][1] - m[1][0] * m[0][1]
    s1 = m[0][0] * m[1][2] - m[1][0] * m[0][2]
    s2 = m[0][0] * m[1][3] - m[1][0] * m[0][3]
    s3 = m[0][1] * m[1][2] - m[1][1] * m[0][2]
    s4 = m[0][1] * m[1][3] - m[1][1] * m[0][3]
    s5 = m[0][2] * m[1][3] - m[1][2] * m[0][3]
    c5 = m[2][2] * m[3][3] - m[3][2] * m[2][3]
    c4 = m[2][1] * m[3][3] - m[3][1] * m[2][3]
    c3 = m[2][1] * m[3][2] - m[3][1] * m[2][2]
    c2 = m[2][0] * m[3][3] - m[3][0] * m[2][3]
    c1 = m[2][0] * m[3][2] - m[3][0] * m[2][2]
    c0 = m[2][0] * m[3][1] - m[3][0] * m[2][1]
    determinant = (s0 * c5 - s1 * c4) + (s2 * c3 + s3 * c2) + (s5 * c0 - s4 * c1)
    b00 = m[1][1] * c5 - m[1][2] * c4 + m[1][3] * c3
    b01 = m[0][2] * c4 - m[0][1] * c5 - m[0][3] * c3
    b02 = m[3][1] * s5 - m[3][2] * s4 + m[3][3] * s3
    b03 = m[2][2] * s4 - m[2][1] * s5 - m[2][3] * s3
    b11 = m[0][0] * c5 - m[0][2] * c2 + m[0][3] * c1
    b12 = m[3][2] * s2 - m[3][0] * s5 - m[3][3] * s1
    b13 = m[2][0] * s5 - m[2][2] * s2 + m[2][3] * s1
    b22 = m[3][0] * s4 - m[3][1] * s2 + m[3][3] * s0
    b23 = m[2][1] * s2 - m[2][0] * s4 - m[2][3] * s0
    b33 = m[2][0] * s3 - m[2][1] * s1 + m[2][2] * s0
    rows = [[b00, b01, b02, b03], [b01, b11, b12, b13], [b02, b12, b22, b23], [b03, b13, b23, b33]]
    return determinant, rows


def solve(both, ids):
    row = lax.broadcasted_iota(jnp.int32, (NDOCS, 128), 0)
    lane = lax.broadcasted_iota(jnp.int32, (NDOCS, 128), 1)
    diagonal = jnp.where(row == lane, both, 0.0)
    trace = jnp.sum(jnp.sum(diagonal, axis=0, keepdims=True), axis=1, keepdims=True)
    a = both / trace + jnp.where(row == lane, 0.1, 0.0)
    for k in range(0, NDOCS, 4):
        r = [a[k + i : k + i + 1, :] for i in range(4)]
        c = [jnp.broadcast_to(a[:, k + i : k + i + 1], (NDOCS, 128)) for i in range(4)]
        m = [[c[j][k + i : k + i + 1] for j in range(4)] for i in range(4)]
        determinant, b = adjugate4(m)
        scale = 1.0 / determinant
        u = [(w[0] * r[0] + w[1] * r[1]) + (w[2] * r[2] + w[3] * r[3]) for w in b]
        rest = a - ((c[0] * u[0] + c[1] * u[1]) + (c[2] * u[2] + c[3] * u[3])) * scale
        for i in range(4):
            rest = jnp.where(row == k + i, u[i] * scale, rest)
        a = rest
    number = lax.broadcasted_iota(jnp.int32, (NDOCS, NDOCS), 0)
    placing = jnp.where(ids == number, 1.0, 0.0)
    return lax.dot_general(
        a[:, 64:96], placing, (((0,), (1,)), ((), ())), precision=HIGH, preferred_element_type=F32
    )


def kernel(
    in_hbm, og_hbm, valid_hbm, blocks_hbm, pin_hbm, pout_hbm, test_hbm, ids_hbm, out_ref,
    tok, grad, valid_ref, blocks_ref, pin_ref, pout_ref, test_ref, ids_ref, w2, w3, pad,
    send_b, recv_b, send_c, recv_c, recv_c2, send_d, recv_d, send_e, recv_e, send_f, recv_f,
    load_sem, gather_send, r2_row, r2, r2_sib, r3, r3_z, r3_sib, phase_send, phase_recv,
):
    dp = lax.axis_index("dp")
    seq = lax.axis_index("seq")
    z, core = dp // 2, lax.rem(dp, 2)
    x, y = seq // NY, lax.rem(seq, NY)

    def shard(i, j):
        return lax.rem(x + i, NX) * NY + lax.rem(y + j, NY)

    def level(k, e):
        return lax.rem(z + k, NZ) * 2 + (core + e * (1 - 2 * core))

    sibling = (level(0, 1), seq)

    barrier = pltpu.get_barrier_semaphore()
    for i, j in PLANE:
        pl.semaphore_signal(barrier, inc=1, device_id=(dp, shard(i, j)), device_id_type=MESH)
    for k, e in STACK:
        pl.semaphore_signal(barrier, inc=1, device_id=(level(k, e), seq), device_id_type=MESH)

    def load(i, src, dst):
        copy = pltpu.make_async_copy(src, dst, load_sem.at[i])
        copy.start()
        return copy

    load_pout = load(0, pout_hbm, pout_ref)
    load_pin = load(1, pin_hbm, pin_ref)
    later = [
        load(2, in_hbm, tok),
        load(3, og_hbm, grad),
        load(4, valid_hbm, valid_ref),
        load(5, blocks_hbm, blocks_ref),
        load(6, test_hbm, test_ref),
        load(7, ids_hbm, ids_ref),
    ]

    def remote(src, dst, send, recv, target):
        return pltpu.make_async_remote_copy(
            src, dst, send, recv, device_id=target, device_id_type=MESH
        )

    def finish(last):
        for sem, part in (
            (0, w2.at[pl.ds(0, 2), pl.ds(0, 5), 0]),
            (1, w2.at[pl.ds(0, NX - 1), pl.ds(0, NY - 1), 0]),
            (2, w2.at[:, :, 0]),
            (3, w3.at[0, 0, pl.ds(0, NSEQ - 1)]),
            (4, w3.at[0, pl.ds(0, 3)]),
            (5, w3.at[0]),
        ):
            remote(part, part, gather_send.at[sem], r2.at[0], sibling).wait_send()
        for phase, buf, count in (
            (0, send_b, NSEQ), (1, recv_c, NDP), (2, recv_c2, NSEQ), (3, recv_d, NSEQ), (4, recv_e, 8),
            (5, recv_f, NDP),
        ):
            if phase <= last:
                part = buf.at[pl.ds(0, count - 1)]
                remote(
                    part, part, phase_send.at[phase], phase_recv.at[phase], sibling
                ).wait_send()

    row = lax.broadcasted_iota(jnp.int32, (64, 64), 0)
    col = lax.broadcasted_iota(jnp.int32, (64, 64), 1)
    source = jnp.where(row < 32, 2 * row, 2 * row - 63)
    order = jnp.where(col == source, 1.0, 0.0).astype(BF16)
    pad[...] = jnp.zeros_like(pad)
    load_pout.wait()
    load_pin.wait()
    pad[:, 0:KO] = jnp.dot(order, pout_ref[...], preferred_element_type=F32)
    even_form = pad[...]
    own_out = jnp.where(lax.rem(seq, 2) == 1, pltpu.roll(even_form, KO, 1), even_form)
    pad[...] = own_out
    last = own_out[:, 384:512]
    last = last + pltpu.roll(last, 64, 1)
    lane = lax.broadcasted_iota(jnp.int32, (32, 128), 1)
    folded = jnp.where(lane < 64, last[0:32], last[32:64]).astype(BF16)
    third, second = own_out[:, 256:384].astype(BF16), pin_ref[...]
    w2[x, y, core, 0:2] = jnp.where(core == 1, third[32:64], third[0:32]).reshape(2, 16, 128)
    w2[x, y, core, 2:4] = jnp.where(core == 1, second[32:64], second[0:32]).reshape(2, 16, 128)
    w2[x, y, core, 4] = jnp.where(core == 1, folded[16:32], folded[0:16])
    part = lax.rem(z, 4)
    quarter = pad[pl.ds(pl.multiple_of(part * 16, 16), 16), 0:256]
    w3[core, part, seq] = jnp.where(core == 1, quarter[:, 128:256], quarter[:, 0:128]).astype(BF16)

    pl.semaphore_wait(barrier, NSEQ - 1 + NDP - 1)

    def column(j):
        return lax.rem(y + j, NY)

    def group_of(i):
        return lax.rem(x + i, NX)

    def pass_on(j):
        piece = w2.at[x, column(j), core]
        remote(piece, piece, gather_send.at[1], r2_row.at[column(j)], sibling).wait_recv()
        for i in X_ORDER:
            recv = r2.at[column(j)]
            remote(piece, piece, gather_send.at[1], recv, (dp, shard(i, 0))).start()

    def collect(*steps):
        for j in steps:
            three = w2.at[pl.ds(0, NX - 1), column(j), core]
            remote(three, three, gather_send.at[2], r2.at[column(j)], sibling).wait_recv()
            four = w2.at[:, column(j), core]
            remote(four, four, gather_send.at[2], r2_sib.at[column(j)], sibling).start()

    def rows_of(group, count=NY):
        return pl.ds(pl.multiple_of(group * NY, NY), count)

    steps = (1, NZ - 1, 2)

    def lift(i):
        group = group_of(i)
        arrived = w3.at[core, part, rows_of(group, NY if i else NY - 1)]
        remote(arrived, arrived, gather_send.at[3], r3.at[group], sibling).wait_recv()
        piece = w3.at[core, part, rows_of(group)]
        for e, step in enumerate(steps):
            far = step if e < 2 else 2 + 4 * core
            target = (lax.rem(z + far, NZ) * 2 + core, seq)
            remote(piece, piece, gather_send.at[4], r3_z.at[group], target).start()

    def land(i):
        group = group_of(i)
        three = w3.at[core, pl.ds(0, 3), rows_of(group)]
        remote(three, three, gather_send.at[4], r3_z.at[group], sibling).wait_recv()
        four = w3.at[core, :, rows_of(group)]
        remote(four, four, gather_send.at[5], r3_sib.at[group], sibling).start()

    def settle_3():
        for group in range(NX):
            four = w3.at[1 - core, :, rows_of(group)]
            remote(four, four, gather_send.at[5], r3_sib.at[group], sibling).wait_recv()

    def settle(step):
        pair = lax.rem(y // 2 + step, NY // 2)
        for q in range(2):
            four = w2.at[:, 2 * pair + q, 1 - core]
            remote(four, four, gather_send.at[2], r2_sib.at[2 * pair + q], sibling).wait_recv()
        return pair

    for i in (0,) + X_ORDER:
        for j in (4, 5, 3, 6, 2, 7, 1) + ((0,) if i else ()):
            piece = w3.at[core, part, seq]
            remote(piece, piece, gather_send.at[3], r3.at[x], (dp, shard(i, j))).start()
    own = w2.at[x, y, core]
    for i in X_ORDER:
        remote(own, own, gather_send.at[0], r2.at[y], (dp, shard(i, 0))).start()
    for j in Y_ORDER:
        remote(own, own, gather_send.at[0], r2_row.at[y], (dp, shard(0, j))).start()

    def product(pair):
        def tiles(i, j):
            k = i * NY + j
            three = [w3[0, :, k], w3[1, :, k], w2[i, j, :, 0:2]]
            return [t.reshape(64, 128) for t in three], w2[i, j, :, 4].reshape(32, 128).astype(F32)

        def columns(ref, width):
            return jnp.concatenate(
                [
                    ref[:, pl.ds(pl.multiple_of((i * NY + 2 * pair) * width, 2 * width), 2 * width)]
                    for i in range(NX)
                ],
                axis=1,
            )

        parts, parts_in = [], []
        for i in range(NX):
            (even, last_even), (odd, last_odd) = tiles(i, 2 * pair), tiles(i, 2 * pair + 1)
            upper = jnp.where(lane < 64, last_even, pltpu.roll(last_odd, 64, 1))
            lower = jnp.where(lane < 64, pltpu.roll(last_even, 64, 1), last_odd)
            joint = jnp.concatenate([upper, lower], axis=0).astype(BF16)
            parts += even + [joint] + odd
            parts_in += [w2[i, 2 * pair + q, :, 2:4].reshape(64, 128) for q in range(2)]
        pg = lax.dot_general(
            jnp.concatenate(parts, axis=1), columns(grad, KO), NT, preferred_element_type=F32
        )
        px = lax.dot_general(
            jnp.concatenate(parts_in, axis=1), columns(tok, KI), NT, preferred_element_type=F32
        )
        return pg, px

    lift(0)
    pass_on(1)
    pass_on(7)
    lift(1)
    lift(3)
    pass_on(2)
    pass_on(6)
    lift(2)
    pass_on(3)
    pass_on(5)
    pass_on(4)
    collect(0, 1, 7)
    for i in (0,) + X_ORDER:
        land(i)
    for copy in later:
        copy.wait()
    collect(2, 6)
    settle_3()
    pg, px = product(settle(0))

    def add(step):
        more_g, more_x = product(settle(step))
        return pg + more_g, px + more_x

    collect(3, 5)
    pg, px = add(1)
    collect(4)
    pg, px = add(3)
    pg, px = add(2)

    pg = jnp.where(valid_ref[...] == 1, pg, 0.0)
    block_grad = lax.dot_general(pg, px, NT, precision=HIGH, preferred_element_type=F32)
    folded = jnp.concatenate([block_grad[0:32], block_grad[32:64]], axis=1)
    send_b[...] = folded.reshape(NSEQ, 1, 128)

    def plane_send(phase, src, dst):
        for i, j in PLANE:
            target = (dp, shard(i, j))
            remote(src(shard(i, j)), dst, phase_send.at[phase], phase_recv.at[phase], target).start()

    def stack_send(phase, src, dst):
        for k, e in STACK:
            target = (level(k, e), seq)
            remote(src, dst, phase_send.at[phase], phase_recv.at[phase], target).start()

    def await_all(phase, buf, count):
        part = buf.at[pl.ds(0, count - 1)]
        remote(part, part, phase_send.at[phase], phase_recv.at[phase], sibling).wait_recv()

    plane_send(0, lambda peer: send_b.at[peer], recv_b.at[seq])
    recv_b[seq] = send_b[seq]
    block = lax.broadcasted_iota(jnp.int32, (NSEQ, 128), 0)
    owner = jnp.zeros((NSEQ, 128), jnp.int32)
    end = 0
    for j in range(4):
        end = end + blocks_ref[0, j]
        owner = owner + jnp.where(block >= end, 1, 0)
    await_all(0, recv_b, NSEQ)
    blocks = recv_b[...].reshape(NSEQ, 128)
    for j in range(4):
        send_c[j : j + 1] = jnp.sum(jnp.where(owner == j, blocks, 0.0), axis=0, keepdims=True)
    stack_send(1, send_c, recv_c.at[dp])
    plane_send(2, lambda peer: send_c, recv_c2.at[seq])
    recv_c[dp] = send_c[...]
    recv_c2[seq] = send_c[...]

    await_all(1, recv_c, NDP)
    every = recv_c[...].reshape(NDOCS, 128)
    eighth = part * 2 + core
    mine = recv_c[pl.ds(eighth * 2, 2)].reshape(8, 128)
    partial = lax.dot_general(mine, every, NT, precision=HIGH, preferred_element_type=F32)
    send_d[...] = jnp.concatenate([partial[0:4], partial[4:8]], axis=1)
    plane_send(3, lambda peer: send_d, recv_d.at[seq])
    recv_d[seq] = send_d[...]

    await_all(2, recv_c2, NSEQ)
    own = jnp.concatenate([recv_c2[t] for t in range(NSEQ)], axis=1)
    high = own.astype(BF16)
    rest = own - high.astype(F32)
    middle = rest.astype(BF16)
    low = (rest - middle.astype(F32)).astype(BF16)
    test = test_ref[...]
    cross = lax.dot_general(high, test, NT, preferred_element_type=F32)
    cross = cross + (
        lax.dot_general(middle, test, NT, preferred_element_type=F32)
        + lax.dot_general(low, test, NT, preferred_element_type=F32)
    )
    send_f[...] = jnp.zeros_like(send_f)
    send_f[:, 64:96] = cross
    stack_send(5, send_f, recv_f.at[dp])
    recv_f[dp] = send_f[...]

    await_all(3, recv_d, NSEQ)
    send_e[...] = jnp.sum(recv_d[...], axis=0)
    for e, step in enumerate(steps):
        far = step if e < 2 else 2 + 4 * core
        for other in range(2):
            target = (lax.rem(z + far, NZ) * 2 + other, seq)
            remote(send_e, recv_e.at[eighth], phase_send.at[4], phase_recv.at[4], target).start()
    remote(send_e, recv_e.at[eighth], phase_send.at[4], phase_recv.at[4], sibling).start()
    recv_e[eighth] = send_e[...]
    finish(5)
    await_all(5, recv_f, NDP)
    await_all(4, recv_e, 8)
    gram = recv_e[...]
    gram = jnp.concatenate([gram, pltpu.roll(gram, 64, 2)], axis=1).reshape(NDOCS, 128)
    lane = lax.broadcasted_iota(jnp.int32, (NDOCS, 128), 1)
    both = jnp.where(lane < NDOCS, gram, recv_f[...].reshape(NDOCS, 128))
    out_ref[...] = solve(both, ids_ref[...])


def exchange(tokens, outgrad, valid, doc_blocks, doc_ids, proj_in, proj_out, test_grads):
    vmem = pl.BlockSpec(memory_space=pltpu.VMEM)
    dma = pltpu.SemaphoreType.DMA
    return pl.pallas_call(
        kernel,
        name="attribution",
        out_shape=jax.ShapeDtypeStruct((32, NDOCS), F32),
        in_specs=[pl.BlockSpec(memory_space=pltpu.HBM)] * 8,
        out_specs=vmem,
        scratch_shapes=[
            pltpu.VMEM((128, 4096), BF16),
            pltpu.VMEM((128, 14336), BF16),
            pltpu.VMEM((1, 128), jnp.int32),
            pltpu.SMEM((1, 4), jnp.int32),
            pltpu.VMEM((64, KI), BF16),
            pltpu.VMEM((64, KO), BF16),
            pltpu.VMEM((32, 4096), BF16),
            pltpu.VMEM((1, NDOCS), jnp.int32),
            pltpu.VMEM((NX, NY, 2, 5, 16, 128), BF16),
            pltpu.VMEM((2, 4, NSEQ, 16, 128), BF16),
            pltpu.VMEM((64, KP), F32),
            pltpu.VMEM((NSEQ, 1, 128), F32),
            pltpu.VMEM((NSEQ, 1, 128), F32),
            pltpu.VMEM((4, 128), F32),
            pltpu.VMEM((NDP, 4, 128), F32),
            pltpu.VMEM((NSEQ, 4, 128), F32),
            pltpu.VMEM((4, 128), F32),
            pltpu.VMEM((NSEQ, 4, 128), F32),
            pltpu.VMEM((4, 128), F32),
            pltpu.VMEM((8, 4, 128), F32),
            pltpu.VMEM((4, 128), F32),
            pltpu.VMEM((NDP, 4, 128), F32),
            dma((8,)),
            dma((6,)),
            dma((NY,)), dma((NY,)), dma((NY,)),
            dma((NX,)), dma((NX,)), dma((NX,)),
            dma((6,)), dma((6,)),
        ],
        compiler_params=pltpu.CompilerParams(
            collective_id=0, has_side_effects=True, vmem_limit_bytes=60 << 20
        ),
    )(tokens, outgrad, valid, doc_blocks, proj_in.T, proj_out.T, test_grads, doc_ids.reshape(1, NDOCS))


def per_device(inputs, out_grads, valid, doc_blocks, doc_ids, proj_in, proj_out, test_grads):
    scaled = exchange(
        inputs[0], out_grads[0], valid, doc_blocks, doc_ids, proj_in, proj_out, test_grads
    )
    return NDOCS * scaled.T


def solution(mesh):
    in_specs = (
        P("dp", "seq", None),
        P("dp", "seq", None),
        P("dp", "seq"),
        P("dp", None),
        P(),
        P("seq", None),
        P("seq", None),
        P("seq", None),
    )
    return jax.shard_map(
        per_device, mesh=mesh, in_specs=in_specs, out_specs=P(None, "seq"), check_vma=False
    )
```

```python
import jax
import jax.numpy as jnp
from jax import lax
from jax.experimental import pallas as pl
from jax.experimental.pallas import tpu as pltpu
from jax.sharding import PartitionSpec as P

MESH = pl.DeviceIdType.MESH
F32 = jnp.float32
BF16 = jnp.bfloat16
HIGH = lax.Precision.HIGHEST
NX, NY, NZ = 4, 8, 8
NSEQ, NDP = NX * NY, 2 * NZ
KO, KP, KI = 448, 512, 128
NDOCS = 64
NT = (((1,), (1,)), ((), ()))
Y_ORDER = (1, 7, 2, 6, 3, 5, 4)
X_ORDER = (1, 3, 2)


def reach(step, size):
    return min(step, size - step)


PLANE = sorted(
    [(i, j) for i in range(NX) for j in range(NY) if i or j],
    key=lambda o: -reach(o[0], NX) - reach(o[1], NY),
)
STACK = sorted(
    [(k, e) for k in range(NZ) for e in range(2) if k or e],
    key=lambda o: -2 * reach(o[0], NZ) - o[1],
)


def adjugate4(m):
    s0 = m[0][0] * m[1][1] - m[1][0] * m[0][1]
    s1 = m[0][0] * m[1][2] - m[1][0] * m[0][2]
    s2 = m[0][0] * m[1][3] - m[1][0] * m[0][3]
    s3 = m[0][1] * m[1][2] - m[1][1] * m[0][2]
    s4 = m[0][1] * m[1][3] - m[1][1] * m[0][3]
    s5 = m[0][2] * m[1][3] - m[1][2] * m[0][3]
    c5 = m[2][2] * m[3][3] - m[3][2] * m[2][3]
    c4 = m[2][1] * m[3][3] - m[3][1] * m[2][3]
    c3 = m[2][1] * m[3][2] - m[3][1] * m[2][2]
    c2 = m[2][0] * m[3][3] - m[3][0] * m[2][3]
    c1 = m[2][0] * m[3][2] - m[3][0] * m[2][2]
    c0 = m[2][0] * m[3][1] - m[3][0] * m[2][1]
    determinant = (s0 * c5 - s1 * c4) + (s2 * c3 + s3 * c2) + (s5 * c0 - s4 * c1)
    b00 = m[1][1] * c5 - m[1][2] * c4 + m[1][3] * c3
    b01 = m[0][2] * c4 - m[0][1] * c5 - m[0][3] * c3
    b02 = m[3][1] * s5 - m[3][2] * s4 + m[3][3] * s3
    b03 = m[2][2] * s4 - m[2][1] * s5 - m[2][3] * s3
    b11 = m[0][0] * c5 - m[0][2] * c2 + m[0][3] * c1
    b12 = m[3][2] * s2 - m[3][0] * s5 - m[3][3] * s1
    b13 = m[2][0] * s5 - m[2][2] * s2 + m[2][3] * s1
    b22 = m[3][0] * s4 - m[3][1] * s2 + m[3][3] * s0
    b23 = m[2][1] * s2 - m[2][0] * s4 - m[2][3] * s0
    b33 = m[2][0] * s3 - m[2][1] * s1 + m[2][2] * s0
    rows = [[b00, b01, b02, b03], [b01, b11, b12, b13], [b02, b12, b22, b23], [b03, b13, b23, b33]]
    return determinant, rows


def solve(both, ids):
    row = lax.broadcasted_iota(jnp.int32, (NDOCS, 128), 0)
    lane = lax.broadcasted_iota(jnp.int32, (NDOCS, 128), 1)
    diagonal = jnp.where(row == lane, both, 0.0)
    trace = jnp.sum(jnp.sum(diagonal, axis=0, keepdims=True), axis=1, keepdims=True)
    a = both / trace + jnp.where(row == lane, 0.1, 0.0)
    for k in range(0, NDOCS, 4):
        r = [a[k + i : k + i + 1, :] for i in range(4)]
        c = [jnp.broadcast_to(a[:, k + i : k + i + 1], (NDOCS, 128)) for i in range(4)]
        m = [[c[j][k + i : k + i + 1] for j in range(4)] for i in range(4)]
        determinant, b = adjugate4(m)
        scale = 1.0 / determinant
        u = [(w[0] * r[0] + w[1] * r[1]) + (w[2] * r[2] + w[3] * r[3]) for w in b]
        rest = a - ((c[0] * u[0] + c[1] * u[1]) + (c[2] * u[2] + c[3] * u[3])) * scale
        for i in range(4):
            rest = jnp.where(row == k + i, u[i] * scale, rest)
        a = rest
    number = lax.broadcasted_iota(jnp.int32, (NDOCS, NDOCS), 0)
    placing = jnp.where(ids == number, 1.0, 0.0)
    return lax.dot_general(
        a[:, 64:96], placing, (((0,), (1,)), ((), ())), precision=HIGH, preferred_element_type=F32
    )


def kernel(
    in_hbm, og_hbm, valid_hbm, blocks_hbm, pin_hbm, pout_hbm, test_hbm, ids_hbm, out_ref,
    tok, grad, valid_ref, blocks_ref, pin_ref, pout_ref, test_ref, ids_ref, w2, w3, pad,
    send_b, recv_b, send_c, recv_c, recv_c2, send_d, recv_d, send_e, recv_e, send_f, recv_f,
    load_sem, gather_send, r2_row, r2, r2_sib, r3, r3_z, r3_sib, phase_send, phase_recv,
):
    dp = lax.axis_index("dp")
    seq = lax.axis_index("seq")
    z, core = dp // 2, lax.rem(dp, 2)
    x, y = seq // NY, lax.rem(seq, NY)

    def shard(i, j):
        return lax.rem(x + i, NX) * NY + lax.rem(y + j, NY)

    def level(k, e):
        return lax.rem(z + k, NZ) * 2 + (core + e * (1 - 2 * core))

    sibling = (level(0, 1), seq)

    barrier = pltpu.get_barrier_semaphore()
    for i, j in PLANE:
        pl.semaphore_signal(barrier, inc=1, device_id=(dp, shard(i, j)), device_id_type=MESH)
    for k, e in STACK:
        pl.semaphore_signal(barrier, inc=1, device_id=(level(k, e), seq), device_id_type=MESH)

    def load(i, src, dst):
        copy = pltpu.make_async_copy(src, dst, load_sem.at[i])
        copy.start()
        return copy

    load_pout = load(0, pout_hbm, pout_ref)
    load_pin = load(1, pin_hbm, pin_ref)
    later = [
        load(2, in_hbm, tok),
        load(3, og_hbm, grad),
        load(4, valid_hbm, valid_ref),
        load(5, blocks_hbm, blocks_ref),
        load(6, test_hbm, test_ref),
        load(7, ids_hbm, ids_ref),
    ]

    def remote(src, dst, send, recv, target):
        return pltpu.make_async_remote_copy(
            src, dst, send, recv, device_id=target, device_id_type=MESH
        )

    def finish(last):
        for sem, part in (
            (0, w2.at[pl.ds(0, 2), pl.ds(0, 5), 0]),
            (1, w2.at[pl.ds(0, NX - 1), pl.ds(0, NY - 1), 0]),
            (2, w2.at[:, :, 0]),
            (3, w3.at[0, 0, 0, pl.ds(0, NY - 1)]),
            (4, w3.at[0, 0, pl.ds(0, NX - 1)]),
            (5, w3.at[0, pl.ds(0, 3)]),
            (6, w3.at[0]),
        ):
            remote(part, part, gather_send.at[sem], r2.at[0], sibling).wait_send()
        for phase, buf, count in (
            (0, send_b, NSEQ), (1, recv_c, NDP), (2, recv_c2, NSEQ), (3, recv_d, NSEQ), (4, recv_e, 8),
            (5, recv_f, NDP),
        ):
            if phase <= last:
                part = buf.at[pl.ds(0, count - 1)]
                remote(
                    part, part, phase_send.at[phase], phase_recv.at[phase], sibling
                ).wait_send()

    row = lax.broadcasted_iota(jnp.int32, (64, 64), 0)
    col = lax.broadcasted_iota(jnp.int32, (64, 64), 1)
    source = jnp.where(row < 32, 2 * row, 2 * row - 63)
    order = jnp.where(col == source, 1.0, 0.0).astype(BF16)
    pad[...] = jnp.zeros_like(pad)
    load_pout.wait()
    load_pin.wait()
    pad[:, 0:KO] = jnp.dot(order, pout_ref[...], preferred_element_type=F32)
    even_form = pad[...]
    own_out = jnp.where(lax.rem(seq, 2) == 1, pltpu.roll(even_form, KO, 1), even_form)
    pad[...] = own_out
    last = own_out[:, 384:512]
    last = last + pltpu.roll(last, 64, 1)
    lane = lax.broadcasted_iota(jnp.int32, (32, 128), 1)
    folded = jnp.where(lane < 64, last[0:32], last[32:64]).astype(BF16)
    third, second = own_out[:, 256:384].astype(BF16), pin_ref[...]
    w2[x, y, core, 0:2] = jnp.where(core == 1, third[32:64], third[0:32]).reshape(2, 16, 128)
    w2[x, y, core, 2:4] = jnp.where(core == 1, second[32:64], second[0:32]).reshape(2, 16, 128)
    w2[x, y, core, 4] = jnp.where(core == 1, folded[16:32], folded[0:16])
    part = lax.rem(z, 4)
    quarter = pad[pl.ds(pl.multiple_of(part * 16, 16), 16), 0:256]
    w3[core, part, x, y] = jnp.where(core == 1, quarter[:, 128:256], quarter[:, 0:128]).astype(BF16)

    pl.semaphore_wait(barrier, NSEQ - 1 + NDP - 1)

    def column(j):
        return lax.rem(y + j, NY)

    def pass_on(j):
        piece = w2.at[x, column(j), core]
        remote(piece, piece, gather_send.at[1], r2_row.at[column(j)], sibling).wait_recv()
        for i in X_ORDER:
            recv = r2.at[column(j)]
            remote(piece, piece, gather_send.at[1], recv, (dp, shard(i, 0))).start()

    def collect(*steps):
        for j in steps:
            three = w2.at[pl.ds(0, NX - 1), column(j), core]
            remote(three, three, gather_send.at[2], r2.at[column(j)], sibling).wait_recv()
            four = w2.at[:, column(j), core]
            remote(four, four, gather_send.at[2], r2_sib.at[column(j)], sibling).start()

    steps = (1, NZ - 1, 2)

    def lift(*columns):
        for j in columns:
            arrived = w3.at[core, part, pl.ds(0, NX if j else NX - 1), column(j)]
            remote(arrived, arrived, gather_send.at[4], r3.at[column(j)], sibling).wait_recv()
            piece = w3.at[core, part, :, column(j)]
            for e, step in enumerate(steps):
                far = step if e < 2 else 2 + 4 * core
                target = (lax.rem(z + far, NZ) * 2 + core, seq)
                remote(piece, piece, gather_send.at[5], r3_z.at[column(j)], target).start()

    def land(*columns):
        for j in columns:
            three = w3.at[core, pl.ds(0, 3), :, column(j)]
            remote(three, three, gather_send.at[5], r3_z.at[column(j)], sibling).wait_recv()
            four = w3.at[core, :, :, column(j)]
            remote(four, four, gather_send.at[6], r3_sib.at[column(j)], sibling).start()

    def settle(step):
        pair = lax.rem(y // 2 + step, NY // 2)
        for q in range(2):
            four = w3.at[1 - core, :, :, 2 * pair + q]
            remote(four, four, gather_send.at[6], r3_sib.at[2 * pair + q], sibling).wait_recv()
            four = w2.at[:, 2 * pair + q, 1 - core]
            remote(four, four, gather_send.at[2], r2_sib.at[2 * pair + q], sibling).wait_recv()
        return pair

    mine = w3.at[core, part, x, y]
    for j in (0,) + Y_ORDER:
        for i in X_ORDER + ((0,) if j else ()):
            target = (dp, shard(i, j))
            remote(mine, mine, gather_send.at[4 if i else 3], r3.at[y], target).start()
    own = w2.at[x, y, core]
    for i in X_ORDER:
        remote(own, own, gather_send.at[0], r2.at[y], (dp, shard(i, 0))).start()
    for j in Y_ORDER:
        remote(own, own, gather_send.at[0], r2_row.at[y], (dp, shard(0, j))).start()

    def product(pair):
        def tiles(i, j):
            three = [w3[0, :, i, j], w3[1, :, i, j], w2[i, j, :, 0:2]]
            return [t.reshape(64, 128) for t in three], w2[i, j, :, 4].reshape(32, 128).astype(F32)

        def columns(ref, width):
            return jnp.concatenate(
                [
                    ref[:, pl.ds(pl.multiple_of((i * NY + 2 * pair) * width, 2 * width), 2 * width)]
                    for i in range(NX)
                ],
                axis=1,
            )

        parts, parts_in = [], []
        for i in range(NX):
            (even, last_even), (odd, last_odd) = tiles(i, 2 * pair), tiles(i, 2 * pair + 1)
            upper = jnp.where(lane < 64, last_even, pltpu.roll(last_odd, 64, 1))
            lower = jnp.where(lane < 64, pltpu.roll(last_even, 64, 1), last_odd)
            joint = jnp.concatenate([upper, lower], axis=0).astype(BF16)
            parts += even + [joint] + odd
            parts_in += [w2[i, 2 * pair + q, :, 2:4].reshape(64, 128) for q in range(2)]
        pg = lax.dot_general(
            jnp.concatenate(parts, axis=1), columns(grad, KO), NT, preferred_element_type=F32
        )
        px = lax.dot_general(
            jnp.concatenate(parts_in, axis=1), columns(tok, KI), NT, preferred_element_type=F32
        )
        return pg, px

    lift(0, 1, 7)
    pass_on(1)
    pass_on(7)
    lift(2, 6)
    pass_on(2)
    pass_on(6)
    lift(3, 5, 4)
    pass_on(3)
    pass_on(5)
    pass_on(4)
    land(0, 1, 7)
    collect(0, 1, 7)
    for copy in later:
        copy.wait()
    land(2, 6)
    collect(2, 6)
    pg, px = product(settle(0))

    def add(step):
        more_g, more_x = product(settle(step))
        return pg + more_g, px + more_x

    land(3, 5)
    collect(3, 5)
    pg, px = add(1)
    land(4)
    collect(4)
    pg, px = add(3)
    pg, px = add(2)

    pg = jnp.where(valid_ref[...] == 1, pg, 0.0)
    block_grad = lax.dot_general(pg, px, NT, precision=HIGH, preferred_element_type=F32)
    folded = jnp.concatenate([block_grad[0:32], block_grad[32:64]], axis=1)
    send_b[...] = folded.reshape(NSEQ, 1, 128)

    def plane_send(phase, src, dst):
        for i, j in PLANE:
            target = (dp, shard(i, j))
            remote(src(shard(i, j)), dst, phase_send.at[phase], phase_recv.at[phase], target).start()

    def stack_send(phase, src, dst):
        for k, e in STACK:
            target = (level(k, e), seq)
            remote(src, dst, phase_send.at[phase], phase_recv.at[phase], target).start()

    def await_all(phase, buf, count):
        part = buf.at[pl.ds(0, count - 1)]
        remote(part, part, phase_send.at[phase], phase_recv.at[phase], sibling).wait_recv()

    plane_send(0, lambda peer: send_b.at[peer], recv_b.at[seq])
    recv_b[seq] = send_b[seq]
    block = lax.broadcasted_iota(jnp.int32, (NSEQ, 128), 0)
    owner = jnp.zeros((NSEQ, 128), jnp.int32)
    end = 0
    for j in range(4):
        end = end + blocks_ref[0, j]
        owner = owner + jnp.where(block >= end, 1, 0)
    await_all(0, recv_b, NSEQ)
    blocks = recv_b[...].reshape(NSEQ, 128)
    for j in range(4):
        send_c[j : j + 1] = jnp.sum(jnp.where(owner == j, blocks, 0.0), axis=0, keepdims=True)
    stack_send(1, send_c, recv_c.at[dp])
    plane_send(2, lambda peer: send_c, recv_c2.at[seq])
    recv_c[dp] = send_c[...]
    recv_c2[seq] = send_c[...]

    await_all(1, recv_c, NDP)
    every = recv_c[...].reshape(NDOCS, 128)
    eighth = part * 2 + core
    mine = recv_c[pl.ds(eighth * 2, 2)].reshape(8, 128)
    partial = lax.dot_general(mine, every, NT, precision=HIGH, preferred_element_type=F32)
    send_d[...] = jnp.concatenate([partial[0:4], partial[4:8]], axis=1)
    plane_send(3, lambda peer: send_d, recv_d.at[seq])
    recv_d[seq] = send_d[...]

    await_all(2, recv_c2, NSEQ)
    own = jnp.concatenate([recv_c2[t] for t in range(NSEQ)], axis=1)
    high = own.astype(BF16)
    rest = own - high.astype(F32)
    middle = rest.astype(BF16)
    low = (rest - middle.astype(F32)).astype(BF16)
    test = test_ref[...]
    cross = lax.dot_general(high, test, NT, preferred_element_type=F32)
    cross = cross + (
        lax.dot_general(middle, test, NT, preferred_element_type=F32)
        + lax.dot_general(low, test, NT, preferred_element_type=F32)
    )
    send_f[...] = jnp.zeros_like(send_f)
    send_f[:, 64:96] = cross
    stack_send(5, send_f, recv_f.at[dp])
    recv_f[dp] = send_f[...]

    await_all(3, recv_d, NSEQ)
    send_e[...] = jnp.sum(recv_d[...], axis=0)
    for e, step in enumerate(steps):
        far = step if e < 2 else 2 + 4 * core
        for other in range(2):
            target = (lax.rem(z + far, NZ) * 2 + other, seq)
            remote(send_e, recv_e.at[eighth], phase_send.at[4], phase_recv.at[4], target).start()
    remote(send_e, recv_e.at[eighth], phase_send.at[4], phase_recv.at[4], sibling).start()
    recv_e[eighth] = send_e[...]
    finish(5)
    await_all(5, recv_f, NDP)
    await_all(4, recv_e, 8)
    gram = recv_e[...]
    gram = jnp.concatenate([gram, pltpu.roll(gram, 64, 2)], axis=1).reshape(NDOCS, 128)
    lane = lax.broadcasted_iota(jnp.int32, (NDOCS, 128), 1)
    both = jnp.where(lane < NDOCS, gram, recv_f[...].reshape(NDOCS, 128))
    out_ref[...] = solve(both, ids_ref[...])


def exchange(tokens, outgrad, valid, doc_blocks, doc_ids, proj_in, proj_out, test_grads):
    vmem = pl.BlockSpec(memory_space=pltpu.VMEM)
    dma = pltpu.SemaphoreType.DMA
    return pl.pallas_call(
        kernel,
        name="attribution",
        out_shape=jax.ShapeDtypeStruct((32, NDOCS), F32),
        in_specs=[pl.BlockSpec(memory_space=pltpu.HBM)] * 8,
        out_specs=vmem,
        scratch_shapes=[
            pltpu.VMEM((128, 4096), BF16),
            pltpu.VMEM((128, 14336), BF16),
            pltpu.VMEM((1, 128), jnp.int32),
            pltpu.SMEM((1, 4), jnp.int32),
            pltpu.VMEM((64, KI), BF16),
            pltpu.VMEM((64, KO), BF16),
            pltpu.VMEM((32, 4096), BF16),
            pltpu.VMEM((1, NDOCS), jnp.int32),
            pltpu.VMEM((NX, NY, 2, 5, 16, 128), BF16),
            pltpu.VMEM((2, 4, NX, NY, 16, 128), BF16),
            pltpu.VMEM((64, KP), F32),
            pltpu.VMEM((NSEQ, 1, 128), F32),
            pltpu.VMEM((NSEQ, 1, 128), F32),
            pltpu.VMEM((4, 128), F32),
            pltpu.VMEM((NDP, 4, 128), F32),
            pltpu.VMEM((NSEQ, 4, 128), F32),
            pltpu.VMEM((4, 128), F32),
            pltpu.VMEM((NSEQ, 4, 128), F32),
            pltpu.VMEM((4, 128), F32),
            pltpu.VMEM((8, 4, 128), F32),
            pltpu.VMEM((4, 128), F32),
            pltpu.VMEM((NDP, 4, 128), F32),
            dma((8,)),
            dma((7,)),
            dma((NY,)), dma((NY,)), dma((NY,)),
            dma((NY,)), dma((NY,)), dma((NY,)),
            dma((6,)), dma((6,)),
        ],
        compiler_params=pltpu.CompilerParams(
            collective_id=0, has_side_effects=True, vmem_limit_bytes=60 << 20
        ),
    )(tokens, outgrad, valid, doc_blocks, proj_in.T, proj_out.T, test_grads, doc_ids.reshape(1, NDOCS))


def per_device(inputs, out_grads, valid, doc_blocks, doc_ids, proj_in, proj_out, test_grads):
    scaled = exchange(
        inputs[0], out_grads[0], valid, doc_blocks, doc_ids, proj_in, proj_out, test_grads
    )
    return NDOCS * scaled.T


def solution(mesh):
    in_specs = (
        P("dp", "seq", None),
        P("dp", "seq", None),
        P("dp", "seq"),
        P("dp", None),
        P(),
        P("seq", None),
        P("seq", None),
        P("seq", None),
    )
    return jax.shard_map(
        per_device, mesh=mesh, in_specs=in_specs, out_specs=P(None, "seq"), check_vma=False
    )
```

```python
import jax
import jax.numpy as jnp
from jax import lax
from jax.experimental import pallas as pl
from jax.experimental.pallas import tpu as pltpu
from jax.sharding import PartitionSpec as P

MESH = pl.DeviceIdType.MESH
F32 = jnp.float32
BF16 = jnp.bfloat16
HIGH = lax.Precision.HIGHEST
NX, NY, NZ = 4, 8, 8
NSEQ, NDP = NX * NY, 2 * NZ
KO, KP, KI = 448, 512, 128
NDOCS = 64
NT = (((1,), (1,)), ((), ()))
Y_ORDER = (1, 7, 2, 6, 3, 5, 4)
X_ORDER = (1, 3, 2)


def reach(step, size):
    return min(step, size - step)


PLANE = sorted(
    [(i, j) for i in range(NX) for j in range(NY) if i or j],
    key=lambda o: -reach(o[0], NX) - reach(o[1], NY),
)
STACK = sorted(
    [(k, e) for k in range(NZ) for e in range(2) if k or e],
    key=lambda o: -2 * reach(o[0], NZ) - o[1],
)


def thirds(a):
    high = a.astype(BF16)
    rest = a - high.astype(F32)
    middle = rest.astype(BF16)
    return high, middle, (rest - middle.astype(F32)).astype(BF16)


def product_nt(a, b):
    (h, m, l), (p, q, r) = thirds(a), thirds(b)
    left = jnp.concatenate([h, h, m, h, l, m], axis=1)
    right = jnp.concatenate([p, q, p, r, p, q], axis=1)
    return lax.dot_general(left, right, NT, preferred_element_type=F32)


def adjugate4(m):
    s0 = m[0][0] * m[1][1] - m[1][0] * m[0][1]
    s1 = m[0][0] * m[1][2] - m[1][0] * m[0][2]
    s2 = m[0][0] * m[1][3] - m[1][0] * m[0][3]
    s3 = m[0][1] * m[1][2] - m[1][1] * m[0][2]
    s4 = m[0][1] * m[1][3] - m[1][1] * m[0][3]
    s5 = m[0][2] * m[1][3] - m[1][2] * m[0][3]
    c5 = m[2][2] * m[3][3] - m[3][2] * m[2][3]
    c4 = m[2][1] * m[3][3] - m[3][1] * m[2][3]
    c3 = m[2][1] * m[3][2] - m[3][1] * m[2][2]
    c2 = m[2][0] * m[3][3] - m[3][0] * m[2][3]
    c1 = m[2][0] * m[3][2] - m[3][0] * m[2][2]
    c0 = m[2][0] * m[3][1] - m[3][0] * m[2][1]
    determinant = (s0 * c5 - s1 * c4) + (s2 * c3 + s3 * c2) + (s5 * c0 - s4 * c1)
    b00 = m[1][1] * c5 - m[1][2] * c4 + m[1][3] * c3
    b01 = m[0][2] * c4 - m[0][1] * c5 - m[0][3] * c3
    b02 = m[3][1] * s5 - m[3][2] * s4 + m[3][3] * s3
    b03 = m[2][2] * s4 - m[2][1] * s5 - m[2][3] * s3
    b11 = m[0][0] * c5 - m[0][2] * c2 + m[0][3] * c1
    b12 = m[3][2] * s2 - m[3][0] * s5 - m[3][3] * s1
    b13 = m[2][0] * s5 - m[2][2] * s2 + m[2][3] * s1
    b22 = m[3][0] * s4 - m[3][1] * s2 + m[3][3] * s0
    b23 = m[2][1] * s2 - m[2][0] * s4 - m[2][3] * s0
    b33 = m[2][0] * s3 - m[2][1] * s1 + m[2][2] * s0
    rows = [[b00, b01, b02, b03], [b01, b11, b12, b13], [b02, b12, b22, b23], [b03, b13, b23, b33]]
    return determinant, rows


def solve(both, ids):
    row = lax.broadcasted_iota(jnp.int32, (NDOCS, 128), 0)
    lane = lax.broadcasted_iota(jnp.int32, (NDOCS, 128), 1)
    diagonal = jnp.where(row == lane, both, 0.0)
    trace = jnp.sum(jnp.sum(diagonal, axis=0, keepdims=True), axis=1, keepdims=True)
    a = both / trace + jnp.where(row == lane, 0.1, 0.0)
    for k in range(0, NDOCS, 4):
        r = [a[k + i : k + i + 1, :] for i in range(4)]
        c = [jnp.broadcast_to(a[:, k + i : k + i + 1], (NDOCS, 128)) for i in range(4)]
        m = [[c[j][k + i : k + i + 1] for j in range(4)] for i in range(4)]
        determinant, b = adjugate4(m)
        scale = 1.0 / determinant
        u = [(w[0] * r[0] + w[1] * r[1]) + (w[2] * r[2] + w[3] * r[3]) for w in b]
        rest = a - ((c[0] * u[0] + c[1] * u[1]) + (c[2] * u[2] + c[3] * u[3])) * scale
        for i in range(4):
            rest = jnp.where(row == k + i, u[i] * scale, rest)
        a = rest
    number = lax.broadcasted_iota(jnp.int32, (NDOCS, NDOCS), 0)
    placing = jnp.where(ids == number, 1.0, 0.0)
    return lax.dot_general(
        a[:, 64:96], placing, (((0,), (1,)), ((), ())), precision=HIGH, preferred_element_type=F32
    )


def kernel(
    in_hbm, og_hbm, valid_hbm, blocks_hbm, pin_hbm, pout_hbm, test_hbm, ids_hbm, out_ref,
    tok, grad, valid_ref, blocks_ref, pin_ref, pout_ref, test_ref, ids_ref, w2, w3, pad,
    send_b, recv_b, send_c, recv_c, recv_c2, send_d, recv_d, send_e, recv_e, send_f, recv_f,
    load_sem, gather_send, r2_row, r2, r2_sib, r3, r3_z, r3_sib, phase_send, phase_recv,
):
    dp = lax.axis_index("dp")
    seq = lax.axis_index("seq")
    z, core = dp // 2, lax.rem(dp, 2)
    x, y = seq // NY, lax.rem(seq, NY)

    def shard(i, j):
        return lax.rem(x + i, NX) * NY + lax.rem(y + j, NY)

    def level(k, e):
        return lax.rem(z + k, NZ) * 2 + (core + e * (1 - 2 * core))

    sibling = (level(0, 1), seq)

    barrier = pltpu.get_barrier_semaphore()
    for i, j in PLANE:
        pl.semaphore_signal(barrier, inc=1, device_id=(dp, shard(i, j)), device_id_type=MESH)
    for k, e in STACK:
        pl.semaphore_signal(barrier, inc=1, device_id=(level(k, e), seq), device_id_type=MESH)

    def load(i, src, dst):
        copy = pltpu.make_async_copy(src, dst, load_sem.at[i])
        copy.start()
        return copy

    load_pout = load(0, pout_hbm, pout_ref)
    load_pin = load(1, pin_hbm, pin_ref)
    later = [
        load(2, in_hbm, tok),
        load(3, og_hbm, grad),
        load(4, valid_hbm, valid_ref),
        load(5, blocks_hbm, blocks_ref),
        load(6, test_hbm, test_ref),
        load(7, ids_hbm, ids_ref),
    ]

    def remote(src, dst, send, recv, target):
        return pltpu.make_async_remote_copy(
            src, dst, send, recv, device_id=target, device_id_type=MESH
        )

    def finish(last):
        for sem, part in (
            (0, w2.at[pl.ds(0, 2), pl.ds(0, 5), 0]),
            (1, w2.at[pl.ds(0, NX - 1), pl.ds(0, NY - 1), 0]),
            (2, w2.at[:, :, 0]),
            (3, w3.at[0, 0, 0, pl.ds(0, NY - 1)]),
            (4, w3.at[0, 0, pl.ds(0, NX - 1)]),
            (5, w3.at[0, pl.ds(0, 3)]),
            (6, w3.at[0]),
        ):
            remote(part, part, gather_send.at[sem], r2.at[0], sibling).wait_send()
        for phase, buf, count in (
            (0, send_b, NSEQ), (1, recv_c, NDP), (2, recv_c2, NSEQ), (3, recv_d, NSEQ), (4, recv_e, 8),
            (5, recv_f, NDP),
        ):
            if phase <= last:
                part = buf.at[pl.ds(0, count - 1)]
                remote(
                    part, part, phase_send.at[phase], phase_recv.at[phase], sibling
                ).wait_send()

    row = lax.broadcasted_iota(jnp.int32, (64, 64), 0)
    col = lax.broadcasted_iota(jnp.int32, (64, 64), 1)
    source = jnp.where(row < 32, 2 * row, 2 * row - 63)
    order = jnp.where(col == source, 1.0, 0.0).astype(BF16)
    pad[...] = jnp.zeros_like(pad)
    load_pout.wait()
    load_pin.wait()
    pad[:, 0:KO] = jnp.dot(order, pout_ref[...], preferred_element_type=F32)
    even_form = pad[...]
    own_out = jnp.where(lax.rem(seq, 2) == 1, pltpu.roll(even_form, KO, 1), even_form)
    pad[...] = own_out
    last = own_out[:, 384:512]
    last = last + pltpu.roll(last, 64, 1)
    lane = lax.broadcasted_iota(jnp.int32, (32, 128), 1)
    folded = jnp.where(lane < 64, last[0:32], last[32:64]).astype(BF16)
    third, second = own_out[:, 256:384].astype(BF16), pin_ref[...]
    w2[x, y, core, 0:2] = jnp.where(core == 1, third[32:64], third[0:32]).reshape(2, 16, 128)
    w2[x, y, core, 2:4] = jnp.where(core == 1, second[32:64], second[0:32]).reshape(2, 16, 128)
    w2[x, y, core, 4] = jnp.where(core == 1, folded[16:32], folded[0:16])
    part = lax.rem(z, 4)
    quarter = pad[pl.ds(pl.multiple_of(part * 16, 16), 16), 0:256]
    w3[core, part, x, y] = jnp.where(core == 1, quarter[:, 128:256], quarter[:, 0:128]).astype(BF16)

    pl.semaphore_wait(barrier, NSEQ - 1 + NDP - 1)

    def column(j):
        return lax.rem(y + j, NY)

    def pass_on(j):
        piece = w2.at[x, column(j), core]
        remote(piece, piece, gather_send.at[1], r2_row.at[column(j)], sibling).wait_recv()
        for i in X_ORDER:
            recv = r2.at[column(j)]
            remote(piece, piece, gather_send.at[1], recv, (dp, shard(i, 0))).start()

    def collect(*steps):
        for j in steps:
            three = w2.at[pl.ds(0, NX - 1), column(j), core]
            remote(three, three, gather_send.at[2], r2.at[column(j)], sibling).wait_recv()
            four = w2.at[:, column(j), core]
            remote(four, four, gather_send.at[2], r2_sib.at[column(j)], sibling).start()

    steps = (1, NZ - 1, 2)

    def lift(*columns):
        for j in columns:
            arrived = w3.at[core, part, pl.ds(0, NX if j else NX - 1), column(j)]
            remote(arrived, arrived, gather_send.at[4], r3.at[column(j)], sibling).wait_recv()
            piece = w3.at[core, part, :, column(j)]
            for e, step in enumerate(steps):
                far = step if e < 2 else 2 + 4 * core
                target = (lax.rem(z + far, NZ) * 2 + core, seq)
                remote(piece, piece, gather_send.at[5], r3_z.at[column(j)], target).start()

    def land(*columns):
        for j in columns:
            three = w3.at[core, pl.ds(0, 3), :, column(j)]
            remote(three, three, gather_send.at[5], r3_z.at[column(j)], sibling).wait_recv()
            four = w3.at[core, :, :, column(j)]
            remote(four, four, gather_send.at[6], r3_sib.at[column(j)], sibling).start()

    def settle(step):
        pair = lax.rem(y // 2 + step, NY // 2)
        for q in range(2):
            four = w3.at[1 - core, :, :, 2 * pair + q]
            remote(four, four, gather_send.at[6], r3_sib.at[2 * pair + q], sibling).wait_recv()
            four = w2.at[:, 2 * pair + q, 1 - core]
            remote(four, four, gather_send.at[2], r2_sib.at[2 * pair + q], sibling).wait_recv()
        return pair

    mine = w3.at[core, part, x, y]
    for j in (0,) + Y_ORDER:
        for i in X_ORDER + ((0,) if j else ()):
            target = (dp, shard(i, j))
            remote(mine, mine, gather_send.at[4 if i else 3], r3.at[y], target).start()
    own = w2.at[x, y, core]
    for i in X_ORDER:
        remote(own, own, gather_send.at[0], r2.at[y], (dp, shard(i, 0))).start()
    for j in Y_ORDER:
        remote(own, own, gather_send.at[0], r2_row.at[y], (dp, shard(0, j))).start()

    def product(pair):
        def tiles(i, j):
            three = [w3[0, :, i, j], w3[1, :, i, j], w2[i, j, :, 0:2]]
            return [t.reshape(64, 128) for t in three], w2[i, j, :, 4].reshape(32, 128).astype(F32)

        def columns(ref, width):
            return jnp.concatenate(
                [
                    ref[:, pl.ds(pl.multiple_of((i * NY + 2 * pair) * width, 2 * width), 2 * width)]
                    for i in range(NX)
                ],
                axis=1,
            )

        parts, parts_in = [], []
        for i in range(NX):
            (even, last_even), (odd, last_odd) = tiles(i, 2 * pair), tiles(i, 2 * pair + 1)
            upper = jnp.where(lane < 64, last_even, pltpu.roll(last_odd, 64, 1))
            lower = jnp.where(lane < 64, pltpu.roll(last_even, 64, 1), last_odd)
            joint = jnp.concatenate([upper, lower], axis=0).astype(BF16)
            parts += even + [joint] + odd
            parts_in += [w2[i, 2 * pair + q, :, 2:4].reshape(64, 128) for q in range(2)]
        pg = lax.dot_general(
            jnp.concatenate(parts, axis=1), columns(grad, KO), NT, preferred_element_type=F32
        )
        px = lax.dot_general(
            jnp.concatenate(parts_in, axis=1), columns(tok, KI), NT, preferred_element_type=F32
        )
        return pg, px

    lift(0, 1, 7)
    pass_on(1)
    pass_on(7)
    lift(2, 6)
    pass_on(2)
    pass_on(6)
    lift(3, 5, 4)
    pass_on(3)
    pass_on(5)
    pass_on(4)
    land(0, 1, 7)
    collect(0, 1, 7)
    for copy in later:
        copy.wait()
    land(2, 6)
    collect(2, 6)
    pg, px = product(settle(0))

    def add(step):
        more_g, more_x = product(settle(step))
        return pg + more_g, px + more_x

    land(3, 5)
    collect(3, 5)
    pg, px = add(1)
    land(4)
    collect(4)
    pg, px = add(3)
    pg, px = add(2)

    pg = jnp.where(valid_ref[...] == 1, pg, 0.0)
    block_grad = product_nt(pg, px)
    folded = jnp.concatenate([block_grad[0:32], block_grad[32:64]], axis=1)
    send_b[...] = folded.reshape(NSEQ, 1, 128)

    def plane_send(phase, src, dst):
        for i, j in PLANE:
            target = (dp, shard(i, j))
            remote(src(shard(i, j)), dst, phase_send.at[phase], phase_recv.at[phase], target).start()

    def stack_send(phase, src, dst):
        for k, e in STACK:
            target = (level(k, e), seq)
            remote(src, dst, phase_send.at[phase], phase_recv.at[phase], target).start()

    def await_all(phase, buf, count):
        part = buf.at[pl.ds(0, count - 1)]
        remote(part, part, phase_send.at[phase], phase_recv.at[phase], sibling).wait_recv()

    plane_send(0, lambda peer: send_b.at[peer], recv_b.at[seq])
    recv_b[seq] = send_b[seq]
    block = lax.broadcasted_iota(jnp.int32, (NSEQ, 128), 0)
    owner = jnp.zeros((NSEQ, 128), jnp.int32)
    end = 0
    for j in range(4):
        end = end + blocks_ref[0, j]
        owner = owner + jnp.where(block >= end, 1, 0)
    await_all(0, recv_b, NSEQ)
    blocks = recv_b[...].reshape(NSEQ, 128)
    for j in range(4):
        send_c[j : j + 1] = jnp.sum(jnp.where(owner == j, blocks, 0.0), axis=0, keepdims=True)
    stack_send(1, send_c, recv_c.at[dp])
    plane_send(2, lambda peer: send_c, recv_c2.at[seq])
    recv_c[dp] = send_c[...]
    recv_c2[seq] = send_c[...]

    await_all(1, recv_c, NDP)
    every = recv_c[...].reshape(NDOCS, 128)
    eighth = part * 2 + core
    mine = recv_c[pl.ds(eighth * 2, 2)].reshape(8, 128)
    partial = product_nt(mine, every)
    send_d[...] = jnp.concatenate([partial[0:4], partial[4:8]], axis=1)
    plane_send(3, lambda peer: send_d, recv_d.at[seq])
    recv_d[seq] = send_d[...]

    await_all(2, recv_c2, NSEQ)
    own = jnp.concatenate([recv_c2[t] for t in range(NSEQ)], axis=1)
    high = own.astype(BF16)
    rest = own - high.astype(F32)
    middle = rest.astype(BF16)
    low = (rest - middle.astype(F32)).astype(BF16)
    test = test_ref[...]
    cross = lax.dot_general(high, test, NT, preferred_element_type=F32)
    cross = cross + (
        lax.dot_general(middle, test, NT, preferred_element_type=F32)
        + lax.dot_general(low, test, NT, preferred_element_type=F32)
    )
    send_f[...] = jnp.zeros_like(send_f)
    send_f[:, 64:96] = cross
    stack_send(5, send_f, recv_f.at[dp])
    recv_f[dp] = send_f[...]

    await_all(3, recv_d, NSEQ)
    send_e[...] = jnp.sum(recv_d[...], axis=0)
    for e, step in enumerate(steps):
        far = step if e < 2 else 2 + 4 * core
        for other in range(2):
            target = (lax.rem(z + far, NZ) * 2 + other, seq)
            remote(send_e, recv_e.at[eighth], phase_send.at[4], phase_recv.at[4], target).start()
    remote(send_e, recv_e.at[eighth], phase_send.at[4], phase_recv.at[4], sibling).start()
    recv_e[eighth] = send_e[...]
    finish(5)
    await_all(5, recv_f, NDP)
    await_all(4, recv_e, 8)
    gram = recv_e[...]
    gram = jnp.concatenate([gram, pltpu.roll(gram, 64, 2)], axis=1).reshape(NDOCS, 128)
    lane = lax.broadcasted_iota(jnp.int32, (NDOCS, 128), 1)
    both = jnp.where(lane < NDOCS, gram, recv_f[...].reshape(NDOCS, 128))
    out_ref[...] = solve(both, ids_ref[...])


def exchange(tokens, outgrad, valid, doc_blocks, doc_ids, proj_in, proj_out, test_grads):
    vmem = pl.BlockSpec(memory_space=pltpu.VMEM)
    dma = pltpu.SemaphoreType.DMA
    return pl.pallas_call(
        kernel,
        name="attribution",
        out_shape=jax.ShapeDtypeStruct((32, NDOCS), F32),
        in_specs=[pl.BlockSpec(memory_space=pltpu.HBM)] * 8,
        out_specs=vmem,
        scratch_shapes=[
            pltpu.VMEM((128, 4096), BF16),
            pltpu.VMEM((128, 14336), BF16),
            pltpu.VMEM((1, 128), jnp.int32),
            pltpu.SMEM((1, 4), jnp.int32),
            pltpu.VMEM((64, KI), BF16),
            pltpu.VMEM((64, KO), BF16),
            pltpu.VMEM((32, 4096), BF16),
            pltpu.VMEM((1, NDOCS), jnp.int32),
            pltpu.VMEM((NX, NY, 2, 5, 16, 128), BF16),
            pltpu.VMEM((2, 4, NX, NY, 16, 128), BF16),
            pltpu.VMEM((64, KP), F32),
            pltpu.VMEM((NSEQ, 1, 128), F32),
            pltpu.VMEM((NSEQ, 1, 128), F32),
            pltpu.VMEM((4, 128), F32),
            pltpu.VMEM((NDP, 4, 128), F32),
            pltpu.VMEM((NSEQ, 4, 128), F32),
            pltpu.VMEM((4, 128), F32),
            pltpu.VMEM((NSEQ, 4, 128), F32),
            pltpu.VMEM((4, 128), F32),
            pltpu.VMEM((8, 4, 128), F32),
            pltpu.VMEM((4, 128), F32),
            pltpu.VMEM((NDP, 4, 128), F32),
            dma((8,)),
            dma((7,)),
            dma((NY,)), dma((NY,)), dma((NY,)),
            dma((NY,)), dma((NY,)), dma((NY,)),
            dma((6,)), dma((6,)),
        ],
        compiler_params=pltpu.CompilerParams(
            collective_id=0, has_side_effects=True, vmem_limit_bytes=60 << 20
        ),
    )(tokens, outgrad, valid, doc_blocks, proj_in.T, proj_out.T, test_grads, doc_ids.reshape(1, NDOCS))


def per_device(inputs, out_grads, valid, doc_blocks, doc_ids, proj_in, proj_out, test_grads):
    scaled = exchange(
        inputs[0], out_grads[0], valid, doc_blocks, doc_ids, proj_in, proj_out, test_grads
    )
    return NDOCS * scaled.T


def solution(mesh):
    in_specs = (
        P("dp", "seq", None),
        P("dp", "seq", None),
        P("dp", "seq"),
        P("dp", None),
        P(),
        P("seq", None),
        P("seq", None),
        P("seq", None),
    )
    return jax.shard_map(
        per_device, mesh=mesh, in_specs=in_specs, out_specs=P(None, "seq"), check_vma=False
    )
```
